256 devices in a mesh: tile: 64 (over y, z, core), depth: 4 (over x).
Axes of the slice: x: 4, y: 4, z: 8, core: 2. Of those that a mesh axis runs over, the one named last changes fastest.
Arguments:
- features: bfloat16 [8192, 128, 128], P('tile'), may hold values from -6 to 6
- geometry: float32 [8192, 6, 128], P('tile'), may hold values from -3 to 4114, as said below
- send_lists: int32 [64, 64, 2], P('tile'), may hold values from 0 to 127, as said below
- tile_ids: int32 [256], P('tile'), may hold values from 0 to 255, as said below
- tile_lists: int32 [256, 8, 8], P('tile', 'depth'), may hold values from 0 to 127, as said below
- live_counts: int32 [256, 8], P('tile', 'depth'), may hold values from 5 to 8, as said below
- cotangent: bfloat16 [256, 256, 128], P('tile'), may hold values from -6 to 6
Outputs:
- image_out: bfloat16 [256, 256, 128], P('tile', 'depth')
- feature_grads: float32 [8192, 128, 128], P('tile', 'depth')
- geometry_grads: float32 [8192, 6, 128], P('tile', None, 'depth')
The draws below stay inside these ranges and needn't reach their ends.
Inputs may be any that keep to these rules, and one draw needn't show every extreme that they name: send_lists[s, t, j] is the local block of owner s in slot j of its bucket for tile index t; the 2 entries of one (s, t) are distinct, and each owner hands out its blocks in a fixed order of its own, repeated, so its blocks are sent equally often up to one. A permutation: tile slot u covers image columns 16 tile_ids[u] to 16 tile_ids[u] + 15 of a band 16 pixels high. tile_lists[u, g, k] = s * 2 + j names block j of the bucket that owner s sends to the tile index holding u; each tile index's 4 * 8 * 8 entries run through an order of its own of its 128 slots, repeated, so every slot is named equally often up to one. Entries at k >= live_counts[u, g] are ignored. `geometry`: Rows: mean x and y in pixels, inverse covariance a, b, c with a > 0, c > 0, a c > b^2, and opacity in (0, 0.9].
All inputs are finite; a program needn't handle non-finite values.
Results may differ from the reference program's by a relative error of at most 0.0085.
Values may be sent and summed in bfloat16 or wider, within the bound.
A program may use at most 64 MiB of HBM per device.

```python
import jax
import jax.numpy as jnp
from jax import lax

FEAT = 128
GB = 128
PIX = 256
CAP = 2
BLK_DEV = 128
TILE_DEV = 4
K = 8
OWNERS = 64
BLOCKS = 8192
TILES = 256
SEGS = 8


def block_plan(key):
    base_key = jax.random.fold_in(key, 4242)
    key_ids, key_perm, key_force, key_pool, key_live, key_spot = jax.random.split(base_key, 6)
    pool_size = OWNERS * CAP
    entries = TILE_DEV * SEGS * K
    tile_order = jax.random.permutation(key_ids, TILES).astype(jnp.int32)
    scores = jax.random.randint(key_perm, (OWNERS, BLK_DEV), 0, 1 << 20) * BLK_DEV + jnp.arange(BLK_DEV, dtype=jnp.int32)[None, :]
    forced = jax.random.randint(key_force, (), 0, OWNERS)
    row_ids = jnp.arange(OWNERS, dtype=jnp.int32)[:, None]
    col_ids = jnp.arange(BLK_DEV, dtype=jnp.int32)[None, :]
    scores = jnp.where((row_ids == forced) & (col_ids == BLK_DEV - 1), -1, scores)
    block_order = jnp.argsort(scores, axis=1).astype(jnp.int32)
    positions = jnp.arange(pool_size, dtype=jnp.int32) % BLK_DEV
    sent = block_order[:, positions].reshape(OWNERS, OWNERS, CAP)
    pool_scores = jax.random.randint(key_pool, (OWNERS, pool_size), 0, 1 << 20) * pool_size + jnp.arange(pool_size, dtype=jnp.int32)[None, :]
    pool_order = jnp.argsort(pool_scores, axis=1).astype(jnp.int32)
    listed = pool_order[:, jnp.arange(entries, dtype=jnp.int32) % pool_size].reshape(TILES, SEGS, K)
    live_table = jax.random.randint(key_live, (TILES, SEGS), K // 2 + 1, K + 1)
    forced_spot = jax.random.randint(key_spot, (), 0, TILES * SEGS)
    live_table = jnp.where(jnp.arange(TILES * SEGS, dtype=jnp.int32).reshape(TILES, SEGS) == forced_spot, K, live_table).astype(jnp.int32)
    return (tile_order, block_order, sent, pool_order, listed, live_table)


def draw_send_lists(key, part):
    return block_plan(key)[2]


def draw_tile_ids(key, part):
    return block_plan(key)[0]


def draw_tile_lists(key, part):
    return block_plan(key)[4]


def draw_live_counts(key, part):
    return block_plan(key)[5]


def draw_geometry(key, part):
    tile_order, block_order, sent, pool_order, listed, live_table = block_plan(key)
    pool_size = OWNERS * CAP
    entries = TILE_DEV * SEGS * K
    block_rank = jnp.argsort(block_order, axis=1).astype(jnp.int32)
    pool_rank = jnp.argsort(pool_order, axis=1).astype(jnp.int32)
    draw_keys = jax.random.split(jax.random.fold_in(key, 99), 8)
    grid_shape = (OWNERS, BLK_DEV, GB)
    first_reps = (pool_size + BLK_DEV - 1) // BLK_DEV
    second_reps = (entries + pool_size - 1) // pool_size
    owner_ids = jnp.arange(OWNERS, dtype=jnp.int32)[:, None, None]
    rank_grid = jnp.broadcast_to(block_rank[:, :, None], grid_shape)
    position = rank_grid + BLK_DEV * jax.random.randint(draw_keys[0], grid_shape, 0, first_reps)
    position = jnp.where(position < pool_size, position, rank_grid)
    sent_flag = (rank_grid < pool_size).astype(jnp.float32)
    position = jnp.minimum(position, pool_size - 1)
    dest_index = position // CAP
    slot_index = owner_ids * CAP + position % CAP
    slot_rank = pool_rank[dest_index, slot_index]
    entry_index = slot_rank + pool_size * jax.random.randint(draw_keys[1], grid_shape, 0, second_reps)
    entry_index = jnp.where(entry_index < entries, entry_index, slot_rank)
    home_tile = dest_index * TILE_DEV + entry_index // (SEGS * K)
    home_seg = entry_index // K % SEGS
    live_flag = (entry_index % K < live_table[home_tile, home_seg]).astype(jnp.float32)
    sigma_low, sigma_high, density = (0.8, 3.0, 40.0)
    sigma_x = jnp.exp(jax.random.uniform(draw_keys[2], grid_shape, jnp.float32, jnp.log(sigma_low), jnp.log(sigma_high)))
    sigma_y = jnp.exp(jax.random.uniform(draw_keys[3], grid_shape, jnp.float32, jnp.log(sigma_low), jnp.log(sigma_high)))
    correlation = jax.random.uniform(draw_keys[4], grid_shape, jnp.float32, -0.6, 0.6)
    squeeze = 1.0 - correlation * correlation
    conic_a = 1.0 / (sigma_x * sigma_x * squeeze)
    conic_b = -correlation / (sigma_x * sigma_y * squeeze)
    conic_c = 1.0 / (sigma_y * sigma_y * squeeze)
    mean_x = 16.0 * tile_order[home_tile].astype(jnp.float32) + jax.random.uniform(draw_keys[5], grid_shape, jnp.float32, -2.0, 18.0)
    mean_y = jax.random.uniform(draw_keys[6], grid_shape, jnp.float32, -2.0, 18.0)
    weight_flat = (sent_flag * live_flag).reshape(-1)
    tile_counts = jax.ops.segment_sum(weight_flat, home_tile.reshape(-1), num_segments=TILES)
    opacity_base = jnp.exp(jax.random.uniform(draw_keys[7], grid_shape, jnp.float32, jnp.log(0.3), jnp.log(3.0)))
    opacity = jnp.minimum(opacity_base * density / jnp.maximum(tile_counts[home_tile], 1.0), 0.9)
    rows_out = [mean_x, mean_y, conic_a, conic_b, conic_c, opacity]
    return jnp.stack([item.reshape(BLOCKS, GB) for item in rows_out], axis=1).astype(jnp.float32)


def shard_levels(stream_key, extent, cuts, low, top_value):
    loudness, own = 1.0, jax.random.fold_in(stream_key, 6)
    for dim, parts in cuts:
        steps = jnp.exp(jax.random.uniform(jax.random.fold_in(own, dim), (parts,), jnp.float32, low / len(cuts), top_value / len(cuts)))
        loudness = loudness * jnp.repeat(steps, extent[dim] // parts).reshape([-1 if axis == dim else 1 for axis in range(len(extent))])
    return loudness


def bell_draw(stream_key, shape, spread, bound, cuts=(), kind=jnp.bfloat16):
    drawn = spread * jax.random.normal(stream_key, shape, jnp.float32)
    if cuts:
        drawn = drawn * shard_levels(stream_key, shape, cuts, -0.22, 0.18)
    return jnp.clip(drawn, -bound, bound).astype(kind)


def setup_inputs(seed: int = 0) -> dict:
    key_of = jax.random.split(jax.random.key(seed), 8)
    return {
        "features": bell_draw(key_of[0], (BLOCKS, GB, FEAT), 1.0, 6.0, ((0, 64),)),
        "geometry": draw_geometry(jax.random.fold_in(key_of[7], 71), 0),
        "send_lists": draw_send_lists(jax.random.fold_in(key_of[7], 71), 0),
        "tile_ids": draw_tile_ids(jax.random.fold_in(key_of[7], 71), 0),
        "tile_lists": draw_tile_lists(jax.random.fold_in(key_of[7], 71), 0),
        "live_counts": draw_live_counts(jax.random.fold_in(key_of[7], 71), 0),
        "cotangent": bell_draw(key_of[6], (TILES, PIX, FEAT), 1.0, 6.0, ((0, 64),)),
    }


def shape_terms(shape_rows, px_row, py_row, live_mask):
    delta_x = px_row[:, None] - shape_rows[0][None, :]
    delta_y = py_row[:, None] - shape_rows[1][None, :]
    conic_a = shape_rows[2][None, :]
    conic_b = shape_rows[3][None, :]
    conic_c = shape_rows[4][None, :]
    quadric = conic_a * delta_x * delta_x + 2.0 * conic_b * delta_x * delta_y + conic_c * delta_y * delta_y
    falloff = jnp.exp(-0.5 * quadric)
    alphas = shape_rows[5][None, :] * falloff * live_mask
    return delta_x, delta_y, conic_a, conic_b, conic_c, falloff, alphas


def reference(features, geometry, send_lists, tile_ids, tile_lists, live_counts, cotangent):
    pixel_iota = jnp.arange(PIX, dtype=jnp.int32)
    column = (pixel_iota % 16).astype(jnp.float32) + 0.5
    row_pos = (pixel_iota // 16).astype(jnp.float32) + 0.5
    entry_iota = jnp.arange(K, dtype=jnp.int32)

    def tile_pass(state_pair, tile_index):
        grad_feat, grad_shape = state_pair
        device = tile_index // TILE_DEV
        slot_ids = tile_lists[tile_index]
        source = slot_ids // CAP
        within = slot_ids % CAP
        block_ids = (source * BLK_DEV + send_lists[source, device, within]).astype(jnp.int32)
        live_rows = (entry_iota[None, :] < live_counts[tile_index][:, None]).astype(jnp.float32)
        px_row = 16.0 * tile_ids[tile_index].astype(jnp.float32) + column
        grads_in = cotangent[tile_index].astype(jnp.float32)

        def seg_forward(block_row, live_row):
            def forward_step(inner, inputs):
                log_light, colors = inner
                block_id, live_mask = inputs
                terms = shape_terms(geometry[block_id], px_row, row_pos, live_mask)
                alphas = terms[6]
                log_keep = jnp.log1p(-alphas)
                inside = jnp.exp(log_light[:, None] + jnp.cumsum(log_keep, axis=1) - log_keep)
                weights = (inside * alphas).astype(jnp.bfloat16)
                colors = colors + jnp.dot(weights, features[block_id], preferred_element_type=jnp.float32)
                return (log_light + jnp.sum(log_keep, axis=1), colors), log_light

            initial = (jnp.zeros((PIX,), jnp.float32), jnp.zeros((PIX, FEAT), jnp.float32))
            (log_light, colors), starts = lax.scan(forward_step, initial, (block_row, live_row))
            return jnp.exp(log_light), colors, starts

        seg_light, seg_color, seg_starts = jax.vmap(seg_forward)(block_ids, live_rows)

        def front_step(light, inputs):
            return light * inputs, light

        _, fronts = lax.scan(front_step, jnp.ones((PIX,), jnp.float32), seg_light)
        image_full = jnp.sum(fronts[:, :, None] * seg_color, axis=0)
        seg_dots = jnp.sum(seg_color * grads_in[None], axis=2)

        def behind_step(suffix, inputs):
            this_light, this_dot = inputs
            return this_dot + this_light * suffix, suffix

        _, behinds = lax.scan(behind_step, jnp.zeros((PIX,), jnp.float32), (seg_light, seg_dots), reverse=True)
        color_grad = (fronts[:, :, None] * grads_in[None]).astype(jnp.bfloat16)
        end_value = fronts * behinds * seg_light

        def seg_backward(block_row, live_row, start_row, color_rows, end_row):
            def backward_step(suffix, inputs):
                block_id, live_mask, log_start = inputs
                block_feat = features[block_id]
                delta_x, delta_y, conic_a, conic_b, conic_c, falloff, alphas = shape_terms(geometry[block_id], px_row, row_pos, live_mask)
                log_keep = jnp.log1p(-alphas)
                inside = jnp.exp(log_start[:, None] + jnp.cumsum(log_keep, axis=1) - log_keep)
                exact_w = inside * alphas
                weights = exact_w.astype(jnp.bfloat16)
                weight_grad = jnp.dot(color_rows, block_feat.T, preferred_element_type=jnp.float32)
                carried = weight_grad * exact_w
                block_total = jnp.sum(carried, axis=1)
                after_sum = suffix[:, None] + block_total[:, None] - jnp.cumsum(carried, axis=1)
                alpha_grad = weight_grad * inside - after_sum / (1.0 - alphas)
                quad_grad = -0.5 * alpha_grad * alphas
                shape_grad = jnp.stack([
                    jnp.sum(-2.0 * quad_grad * (conic_a * delta_x + conic_b * delta_y), axis=0),
                    jnp.sum(-2.0 * quad_grad * (conic_b * delta_x + conic_c * delta_y), axis=0),
                    jnp.sum(quad_grad * delta_x * delta_x, axis=0),
                    jnp.sum(2.0 * quad_grad * delta_x * delta_y, axis=0),
                    jnp.sum(quad_grad * delta_y * delta_y, axis=0),
                    jnp.sum(alpha_grad * falloff * live_mask, axis=0)], axis=0)
                feat_grad = jnp.dot(weights.T, color_rows, preferred_element_type=jnp.float32)
                return suffix + block_total, (feat_grad, shape_grad)

            _, results = lax.scan(backward_step, end_row, (block_row, live_row, start_row), reverse=True)
            return results

        feat_grads, shape_grads = jax.vmap(seg_backward)(block_ids, live_rows, seg_starts, color_grad, end_value)
        flat_ids = block_ids.reshape(SEGS * K)
        grad_feat = grad_feat.at[flat_ids].add(feat_grads.reshape(SEGS * K, GB, FEAT))
        grad_shape = grad_shape.at[flat_ids].add(shape_grads.reshape(SEGS * K, 6, GB))
        return (grad_feat, grad_shape), image_full.astype(jnp.bfloat16)

    initial = (jnp.zeros((BLOCKS, GB, FEAT), jnp.float32), jnp.zeros((BLOCKS, 6, GB), jnp.float32))
    (grad_feat, grad_shape), images = lax.scan(tile_pass, initial, jnp.arange(TILES, dtype=jnp.int32))
    return images, grad_feat, grad_shape
```

```python
import functools

import jax
import jax.numpy as jnp
from jax import lax
from jax.experimental import pallas as pl
from jax.experimental.pallas import tpu as pltpu
from jax.sharding import PartitionSpec as P

MESH = pl.DeviceIdType.MESH
F32 = jnp.float32
BF16 = jnp.bfloat16
I32 = jnp.int32


def iota(shape, dim):
    return lax.broadcasted_iota(I32, shape, dim)


def ones_where(mask):
    return jnp.where(mask, 1.0, 0.0).astype(BF16)


def split_two(value):
    high = value.astype(BF16)
    low = (value - high.astype(F32)).astype(BF16)
    return high, low


def splat_kernel(
    nt,
    nd,
    cap,
    features,
    geo_own,
    lists_own,
    picked,
    tile_ids,
    cot,
    image_out,
    grad_rx,
    ggeo_rx,
    own_feat,
    feat_tx,
    feat_rx,
    feat_list,
    geo_tx,
    geo_rx,
    lists_rx,
    inv_vec,
    lists_sm,
    inv_sm,
    geo_part,
    geo,
    fall,
    chain,
    later,
    weights,
    light_rx,
    carry_rx,
    offs,
    grad_list,
    grad_tx,
    ggeo,
    ggeo_list,
    ggeo_tx,
    image_part,
    image_rx,
    local_sem,
    geo_sem,
    feat_sem,
    grad_sem,
    ggeo_sem,
    lists_send,
    lists_recv,
    light_send,
    light_recv,
    carry_send,
    carry_recv,
    image_send,
    image_recv,
):
    me = lax.axis_index("tile")
    my = lax.axis_index("depth")
    slots = nt * cap

    barrier = pltpu.get_barrier_semaphore()

    def greet(i, c):
        pl.semaphore_signal(
            barrier, inc=1, device_id={"tile": lax.rem(me + i, nt)}, device_id_type=MESH
        )
        return c

    lax.fori_loop(1, nt, greet, 0)
    for step in range(1, nd):
        pl.semaphore_signal(
            barrier, inc=1, device_id={"depth": lax.rem(my + step, nd)}, device_id_type=MESH
        )

    fetch = pltpu.make_async_copy(
        features.at[:, pl.ds(pl.multiple_of(my * 32, 32), 32), :], own_feat, local_sem.at[0]
    )
    fetch.start()

    def pick_geo(k, c):
        geo_tx[k] = geo_own[picked[k]]
        return c

    lax.fori_loop(0, slots, pick_geo, 0, unroll=8)
    mine = pl.multiple_of(me * cap, cap)
    geo_rx[pl.ds(mine, cap)] = geo_tx[pl.ds(mine, cap)]
    lists_rx[my] = lists_own[...]
    fetch.wait()

    def pick_feat(k, c):
        feat_tx[k] = own_feat[picked[k]]
        return c

    lax.fori_loop(0, slots, pick_feat, 0, unroll=8)
    feat_rx[pl.ds(mine, cap)] = feat_tx[pl.ds(mine, cap)]
    for par in range(2):
        light_rx[par, my] = jnp.zeros((256, 128), F32)
        carry_rx[par, my] = jnp.zeros((256, 128), F32)
    image_part[...] = jnp.zeros(image_part.shape, F32)

    pl.semaphore_wait(barrier, nt - 1 + nd - 1)

    def across_depth(source, target, send, recv, step):
        peer = lax.rem(my + step, nd)
        return pltpu.make_async_remote_copy(
            src_ref=source(peer),
            dst_ref=target,
            send_sem=send.at[peer],
            recv_sem=recv.at[my],
            device_id={"depth": peer},
            device_id_type=MESH,
        )

    def arrived_depth(buffer, send, recv, step):
        other = lax.rem(my + step, nd)
        return pltpu.make_async_remote_copy(
            src_ref=buffer(other),
            dst_ref=buffer(other),
            send_sem=send.at[other],
            recv_sem=recv.at[other],
            device_id={"depth": other},
            device_id_type=MESH,
        )

    def scatter_tiles(source, target, sem):
        def send(i, c):
            peer = lax.rem(me + i, nt)
            there = pl.multiple_of(peer * cap, cap)
            pltpu.make_async_remote_copy(
                src_ref=source.at[pl.ds(there, cap)],
                dst_ref=target.at[pl.ds(mine, cap)],
                send_sem=sem.at[0],
                recv_sem=sem.at[1],
                device_id={"tile": peer},
                device_id_type=MESH,
            ).start()
            return c

        lax.fori_loop(1, nt, send, 0)

    def all_tiles(source, target, sem):
        many = (nt - 1) * cap
        return pltpu.make_async_remote_copy(
            src_ref=source.at[pl.ds(0, many)],
            dst_ref=target.at[pl.ds(0, many)],
            send_sem=sem.at[0],
            recv_sem=sem.at[1],
            device_id={"tile": lax.rem(me + 1, nt)},
            device_id_type=MESH,
        )

    for step in range(1, nd):
        across_depth(lambda q: lists_rx.at[my], lists_rx.at[my], lists_send, lists_recv, step).start()
    scatter_tiles(geo_tx, geo_rx, geo_sem)
    scatter_tiles(feat_tx, feat_rx, feat_sem)

    for step in range(1, nd):
        arrived_depth(lambda q: lists_rx.at[q], lists_send, lists_recv, step).wait_recv()
    to_scalar = pltpu.make_async_copy(lists_rx, lists_sm, local_sem.at[1])
    to_scalar.start()
    slot_of_row = iota((128, 128), 0)
    lane = iota((128, 128), 1)
    found = jnp.zeros((128, 128), I32)
    for q in range(nd):
        row = jnp.broadcast_to(lists_rx[q, 0:1, :], (128, 128))
        hit = (row == slot_of_row) & (lane < 32)
        found = found + jnp.where(hit, lane + 32 * q, 0)
    for shift in (64, 32, 16, 8, 4, 2, 1):
        found = found + pltpu.roll(found, shift, 1)
    inv_vec[...] = jnp.transpose(found)[0:8]
    to_scalar.wait()
    inv_copy = pltpu.make_async_copy(inv_vec, inv_sm, local_sem.at[2])
    inv_copy.start()

    def within(index):
        return jnp.clip(index, 0, slots - 1)

    def slot_at(par, g, k):
        return within(lists_sm[g // 2, 0, par * 16 + (g % 2) * 8 + k])

    def live_at(tile, g):
        return lists_sm[g // 2, 0, 64 + tile * 2 + g % 2]

    all_tiles(geo_tx, geo_rx, geo_sem).wait_recv()

    def sort_geo(at, c):
        for k in range(8):
            rows = geo_rx[slot_at(at // 8, at % 8, k)]
            group = at * 2 + k // 4
            for r in range(2):
                geo_part[r, k % 4, pl.ds(group, 1), :] = rows[r : r + 1, :]
        return c

    lax.fori_loop(0, 16, sort_geo, 0)
    lane_part = iota((32, 128), 1) // 32
    for p in range(6):
        r, m = p // 4, p % 4
        total = jnp.zeros((32, 128), F32)
        for i in range(4):
            shift = (32 * (i - m)) % 128
            part = geo_part[r, i]
            moved = pltpu.roll(part, shift, 1) if shift else part
            total = jnp.where(lane_part == i, moved, total)
        geo[p] = total

    row_in = iota((256, 128), 0) % 128
    lane_out = iota((256, 128), 1)
    same_block = row_in // 32 == lane_out // 32
    before_mat = ones_where(same_block & (row_in < lane_out))
    after_mat = ones_where(same_block & (row_in > lane_out))
    place_key = lane_out - row_in // 32
    column = iota((16, 128), 0).astype(F32) + 0.5
    entry_lane = iota((16, 128), 1) // 32

    def placing(base):
        return ones_where(place_key == base)

    def row_of(p, group):
        return jnp.broadcast_to(geo[p, pl.ds(group, 1), :], (16, 128))

    def origin(tile):
        return 16.0 * tile_ids[tile].astype(F32)

    def joined(pieces):
        return jnp.concatenate(pieces, axis=0)

    in_lane = iota((128, 256), 0)
    in_entry = in_lane % 64
    in_high = in_lane // 64
    out_entry = iota((128, 256), 1) // 32

    def offset_mat(high, g, later_ones):
        want = out_entry + g * 8
        key = jnp.where(in_high == high, in_entry, -1000 if later_ones else 1000)
        strict = key > want if later_ones else key < want
        pair = jnp.concatenate([ones_where(strict), ones_where(key == want)], axis=0)
        return jnp.concatenate([pair, pair], axis=0)

    def offsets_from(buffer, par, later_ones):
        total = buffer[par, 0] + buffer[par, 1] + buffer[par, 2] + buffer[par, 3]
        partial = jnp.zeros((256, 128), F32)
        for q in range(nd):
            counts = my < q if later_ones else my > q
            partial = partial + jnp.where(counts, 1.0, 0.0) * buffer[par, q]
        total_high, total_low = split_two(total)
        part_high, part_low = split_two(partial)
        offs[...] = jnp.concatenate([total_high, part_high, total_low, part_low], axis=1)

    for par in range(2):

        def alpha_step(g, c, par=par):
            for h in range(2):
                group = (par * 8 + g) * 2 + h
                mean_x, mean_y = row_of(0, group), row_of(1, group)
                half_a = -0.5 * row_of(2, group)
                minus_b = -row_of(3, group)
                half_c = -0.5 * row_of(4, group)
                opacity = row_of(5, group)
                for high in range(2):
                    tile = high * 2 + par
                    dx = column - (mean_x - origin(tile))
                    alive = entry_lane + h * 4 < live_at(tile, g)
                    ax = jnp.where(alive, half_a * dx * dx, -1e30)
                    highs, lows = [], []
                    for py in range(16):
                        dy = (py + 0.5) - mean_y
                        power = dx * (minus_b * dy) + (ax + half_c * dy * dy)
                        falloff = jnp.exp(power)
                        fall[tile, g * 2 + h, pl.ds(py * 16, 16), :] = falloff
                        log_keep = jnp.log(1.0 - opacity * falloff)
                        top, rest = split_two(log_keep)
                        highs.append(top)
                        lows.append(rest)
                    both = jnp.concatenate([joined(highs), joined(lows)], axis=1)
                    right = jnp.concatenate(
                        [before_mat, placing(high * 64 + g * 8 + h * 4)], axis=1
                    )
                    sums = jnp.dot(both, right, preferred_element_type=F32)
                    chain[tile, g * 2 + h] = sums[:, :128]
                    light_rx[par, my] += sums[:, 128:]
            return c

        lax.fori_loop(0, 8, alpha_step, 0)
        for step in range(1, nd):
            across_depth(
                lambda q: light_rx.at[par, my],
                light_rx.at[par, my],
                light_send.at[par],
                light_recv.at[par],
                step,
            ).start()

    inv_copy.wait()

    for par in range(2):
        for step in range(1, nd):
            arrived_depth(
                lambda q: light_rx.at[par, q], light_send.at[par], light_recv.at[par], step
            ).wait_recv()
        offsets_from(light_rx, par, False)

        def weight_step(g, c, par=par):
            grad = jnp.zeros((256, 128), F32)
            for high in range(2):
                tile = high * 2 + par
                ahead = jnp.dot(
                    offs[...], offset_mat(high, g, False), preferred_element_type=F32
                )
                halves = []
                for h in range(2):
                    group = (par * 8 + g) * 2 + h
                    opacity = jnp.broadcast_to(geo[5, pl.ds(group, 1), :], (256, 128))
                    through = jnp.exp(
                        chain[tile, g * 2 + h] + ahead[:, h * 128 : (h + 1) * 128]
                    )
                    chain[tile, g * 2 + h] = through
                    halves.append((through * (opacity * fall[tile, g * 2 + h])).astype(BF16))
                weight = jnp.concatenate(halves, axis=1)
                weights[tile, g] = weight
                grad = grad + lax.dot_general(
                    weight, cot[tile], (((0,), (0,)), ((), ())), preferred_element_type=F32
                )
            at = (g // 2) * 4 + par * 2 + g % 2
            grad_list[pl.ds(pl.multiple_of(at * 8, 8), 8)] = grad.astype(BF16).reshape(8, 32, 128)
            return c

        lax.fori_loop(0, 8, weight_step, 0)

    def back_feat(k, c):
        grad_tx[k] = grad_list[within(inv_sm[0, k])]
        return c

    lax.fori_loop(0, slots, back_feat, 0, unroll=8)
    keep_own = pltpu.make_async_copy(
        grad_tx.at[pl.ds(mine, cap)], grad_rx.at[pl.ds(mine, cap)], local_sem.at[3]
    )
    keep_own.start()
    all_tiles(feat_tx, feat_rx, feat_sem).wait_recv()
    scatter_tiles(grad_tx, grad_rx, grad_sem)

    def sort_feat(at, c):
        for k in range(8):
            feat_list[at, pl.ds(k * 32, 32), :] = feat_rx[slot_at(at // 8, at % 8, k)]
        return c

    lax.fori_loop(0, 16, sort_feat, 0)

    for par in range(2):

        def carry_step(g, c, par=par):
            feat = feat_list[par * 8 + g]
            for high in range(2):
                tile = high * 2 + par
                image_part[tile] += jnp.dot(weights[tile, g], feat, preferred_element_type=F32)
                dots = lax.dot_general(
                    cot[tile], feat, (((1,), (1,)), ((), ())), preferred_element_type=F32
                )
                for h in range(2):
                    group = (par * 8 + g) * 2 + h
                    opacity = jnp.broadcast_to(geo[5, pl.ds(group, 1), :], (256, 128))
                    direct = dots[:, h * 128 : (h + 1) * 128] * chain[tile, g * 2 + h]
                    chain[tile, g * 2 + h] = direct
                    carried = direct * (opacity * fall[tile, g * 2 + h])
                    top, rest = split_two(carried)
                    both = jnp.concatenate([top, rest], axis=1)
                    right = jnp.concatenate(
                        [after_mat, placing(high * 64 + g * 8 + h * 4)], axis=1
                    )
                    sums = jnp.dot(both, right, preferred_element_type=F32)
                    later[tile, g * 2 + h] = sums[:, :128]
                    carry_rx[par, my] += sums[:, 128:]
            return c

        lax.fori_loop(0, 8, carry_step, 0)
        for step in range(1, nd):
            across_depth(
                lambda q: carry_rx.at[par, my],
                carry_rx.at[par, my],
                carry_send.at[par],
                carry_recv.at[par],
                step,
            ).start()
    for step in range(1, nd):
        across_depth(
            lambda q: image_part.at[:, pl.ds(pl.multiple_of(q * 64, 64), 64), :],
            image_rx.at[my],
            image_send,
            image_recv,
            step,
        ).start()

    for par in range(2):
        for step in range(1, nd):
            arrived_depth(
                lambda q: carry_rx.at[par, q], carry_send.at[par], carry_recv.at[par], step
            ).wait_recv()
        offsets_from(carry_rx, par, True)

        def shape_step(g, c, par=par):
            behind = [
                jnp.dot(offs[...], offset_mat(high, g, True), preferred_element_type=F32)
                for high in range(2)
            ]
            for h in range(2):
                group = (par * 8 + g) * 2 + h
                mean_x, mean_y = row_of(0, group), row_of(1, group)
                opacity = row_of(5, group)
                moments = [jnp.zeros((16, 128), F32) for _ in range(6)]
                for high in range(2):
                    tile = high * 2 + par
                    dx = column - (mean_x - origin(tile))
                    flat = jnp.zeros((16, 128), F32)
                    tilt = jnp.zeros((16, 128), F32)
                    bend = jnp.zeros((16, 128), F32)
                    for py in range(16):
                        rows = pl.ds(py * 16, 16)
                        dy = (py + 0.5) - mean_y
                        falloff = fall[tile, g * 2 + h, rows, :]
                        after = (
                            later[tile, g * 2 + h, rows, :]
                            + behind[high][py * 16 : py * 16 + 16, h * 128 : (h + 1) * 128]
                        )
                        alpha_grad = chain[tile, g * 2 + h, rows, :] - after / (
                            1.0 - opacity * falloff
                        )
                        term = alpha_grad * falloff
                        term_y = term * dy
                        flat = flat + term
                        tilt = tilt + term_y
                        bend = bend + term_y * dy
                    flat_x = flat * dx
                    adds = [flat, flat_x, tilt, flat_x * dx, tilt * dx, bend]
                    moments = [a + b for a, b in zip(moments, adds)]
                one, sx, sy, sxx, sxy, syy = [
                    jnp.sum(m, axis=0, keepdims=True) for m in moments
                ]
                conic_a, conic_b, conic_c, opac = [
                    geo[p, pl.ds(group, 1), :] for p in (2, 3, 4, 5)
                ]
                ggeo[0, pl.ds(group, 1), :] = opac * (conic_a * sx + conic_b * sy)
                ggeo[1, pl.ds(group, 1), :] = opac * (conic_b * sx + conic_c * sy)
                ggeo[2, pl.ds(group, 1), :] = -0.5 * opac * sxx
                ggeo[3, pl.ds(group, 1), :] = -opac * sxy
                ggeo[4, pl.ds(group, 1), :] = -0.5 * opac * syy
                ggeo[5, pl.ds(group, 1), :] = one
            return c

        lax.fori_loop(0, 8, shape_step, 0)

    for i in range(4):
        for r in range(2):
            total = jnp.zeros((32, 128), F32)
            for m in range(4 if r == 0 else 2):
                shift = (32 * (m - i)) % 128
                part = ggeo[4 * r + m]
                moved = pltpu.roll(part, shift, 1) if shift else part
                total = jnp.where(lane_part == m, moved, total)
            ggeo_list[r, i] = total

    def back_geo(k, c):
        at = within(inv_sm[0, k])
        g = (at // 32) * 2 + (at // 8) % 2
        group = (((at // 16) % 2) * 8 + g) * 2 + (at % 8) // 4
        first = ggeo_list[0, at % 4, pl.ds(group, 1), :]
        second = ggeo_list[1, at % 4, pl.ds(group, 1), :]
        ggeo_tx[k] = jnp.concatenate([first, second], axis=0)
        return c

    lax.fori_loop(0, slots, back_geo, 0, unroll=8)
    keep_geo = pltpu.make_async_copy(
        ggeo_tx.at[pl.ds(mine, cap)], ggeo_rx.at[pl.ds(mine, cap)], local_sem.at[4]
    )
    keep_geo.start()
    scatter_tiles(ggeo_tx, ggeo_rx, ggeo_sem)

    image = image_part[:, pl.ds(pl.multiple_of(my * 64, 64), 64), :]
    for step in range(1, nd):
        arrived_depth(lambda q: image_rx.at[q], image_send, image_recv, step).wait_recv()
    for step in range(1, nd):
        image = image + image_rx[lax.rem(my + step, nd)]
    image_out[...] = image.astype(BF16)

    for step in range(1, nd):
        arrived_depth(lambda q: lists_rx.at[q], lists_send, lists_recv, step).wait_send()
        arrived_depth(lambda q: image_rx.at[q], image_send, image_recv, step).wait_send()
        for par in range(2):
            arrived_depth(
                lambda q: light_rx.at[par, q], light_send.at[par], light_recv.at[par], step
            ).wait_send()
            arrived_depth(
                lambda q: carry_rx.at[par, q], carry_send.at[par], carry_recv.at[par], step
            ).wait_send()
    all_tiles(geo_tx, geo_rx, geo_sem).wait_send()
    all_tiles(feat_tx, feat_rx, feat_sem).wait_send()
    keep_own.wait()
    keep_geo.wait()
    all_tiles(grad_tx, grad_rx, grad_sem).wait()
    all_tiles(ggeo_tx, ggeo_rx, ggeo_sem).wait()


def owner_kernel(picked, grad_rx, ggeo_rx, grad_out, ggeo_out):
    def put(k, c):
        at = picked[k]
        grad_out[at] = grad_rx[k].astype(F32)
        ggeo_out[at] = ggeo_rx[k]
        return c

    lax.fori_loop(0, grad_rx.shape[0], put, 0, unroll=8)


def local(features, geometry, send_lists, tile_ids, tile_lists, live_counts, cotangent):
    nt, nd = lax.axis_size("tile"), lax.axis_size("depth")
    my = lax.axis_index("depth")
    cap = send_lists.shape[2]
    slots = nt * cap
    blocks = features.shape[0]
    picked = send_lists.reshape(slots)
    quarter = lax.dynamic_slice_in_dim(geometry, my * 32, 32, 2)
    geo_own = jnp.pad(quarter, ((0, 0), (0, 2), (0, 0))).reshape(blocks, 2, 128)
    row = jnp.concatenate(
        [tile_lists.reshape(64), live_counts.reshape(8), jnp.zeros((56,), I32)]
    )
    lists_own = jnp.broadcast_to(row[None, :], (8, 128))

    vmem = pl.BlockSpec(memory_space=pltpu.VMEM)
    smem = pl.BlockSpec(memory_space=pltpu.SMEM)
    hbm = pl.BlockSpec(memory_space=pl.ANY)
    dma = pltpu.SemaphoreType.DMA
    image_out, grad_rx, ggeo_rx = pl.pallas_call(
        functools.partial(splat_kernel, nt, nd, cap),
        out_shape=(
            jax.ShapeDtypeStruct((4, 64, 128), BF16),
            jax.ShapeDtypeStruct((slots, 32, 128), BF16),
            jax.ShapeDtypeStruct((slots, 2, 128), F32),
        ),
        in_specs=[hbm, vmem, vmem, smem, smem, vmem],
        out_specs=(vmem, hbm, hbm),
        scratch_shapes=[
            pltpu.VMEM((blocks, 32, 128), BF16),
            pltpu.VMEM((slots, 32, 128), BF16),
            pltpu.VMEM((slots, 32, 128), BF16),
            pltpu.VMEM((16, 256, 128), BF16),
            pltpu.VMEM((slots, 2, 128), F32),
            pltpu.VMEM((slots, 2, 128), F32),
            pltpu.VMEM((nd, 8, 128), I32),
            pltpu.VMEM((8, 128), I32),
            pltpu.SMEM((nd, 8, 128), I32),
            pltpu.SMEM((8, 128), I32),
            pltpu.VMEM((2, 4, 32, 128), F32),
            pltpu.VMEM((6, 32, 128), F32),
            pltpu.VMEM((4, 16, 256, 128), F32),
            pltpu.VMEM((4, 16, 256, 128), F32),
            pltpu.VMEM((4, 16, 256, 128), F32),
            pltpu.VMEM((4, 8, 256, 256), BF16),
            pltpu.VMEM((2, nd, 256, 128), F32),
            pltpu.VMEM((2, nd, 256, 128), F32),
            pltpu.VMEM((256, 512), BF16),
            pltpu.VMEM((slots, 32, 128), BF16),
            pltpu.VMEM((slots, 32, 128), BF16),
            pltpu.VMEM((6, 32, 128), F32),
            pltpu.VMEM((2, 4, 32, 128), F32),
            pltpu.VMEM((slots, 2, 128), F32),
            pltpu.VMEM((4, 256, 128), F32),
            pltpu.VMEM((nd, 4, 64, 128), F32),
            dma((5,)),
            dma((2,)),
            dma((2,)),
            dma((2,)),
            dma((2,)),
            dma((nd,)),
            dma((nd,)),
            dma((2, nd)),
            dma((2, nd)),
            dma((2, nd)),
            dma((2, nd)),
            dma((nd,)),
            dma((nd,)),
        ],
        compiler_params=pltpu.CompilerParams(
            collective_id=0, has_side_effects=True, vmem_limit_bytes=62 * 1024 * 1024
        ),
        name="splat",
    )(features, geo_own, lists_own, picked, tile_ids, cotangent)

    feature_grads, ggeo = pl.pallas_call(
        owner_kernel,
        out_shape=(
            jax.ShapeDtypeStruct((blocks, 32, 128), F32),
            jax.ShapeDtypeStruct((blocks, 2, 128), F32),
        ),
        in_specs=[smem, vmem, vmem],
        out_specs=(vmem, vmem),
        name="owner",
    )(picked, grad_rx, ggeo_rx)
    geometry_grads = ggeo.reshape(blocks, 8, 32)[:, :6]
    return image_out, feature_grads, geometry_grads


def solution(mesh):
    placed = (
        P("tile", None, None),
        P("tile", None, None),
        P("tile", None, None),
        P("tile"),
        P("tile", "depth", None),
        P("tile", "depth"),
        P("tile", None, None),
    )
    return jax.shard_map(
        local,
        mesh=mesh,
        in_specs=placed,
        out_specs=(P("tile", "depth", None), P("tile", "depth", None), P("tile", None, "depth")),
        check_vma=False,
    )
```

```python
import functools

import jax
import jax.numpy as jnp
from jax import lax
from jax.experimental import pallas as pl
from jax.experimental.pallas import tpu as pltpu
from jax.sharding import PartitionSpec as P

MESH = pl.DeviceIdType.MESH
F32 = jnp.float32
BF16 = jnp.bfloat16
I32 = jnp.int32


def iota(shape, dim):
    return lax.broadcasted_iota(I32, shape, dim)


def ones_where(mask):
    return jnp.where(mask, 1.0, 0.0).astype(BF16)


def split_two(value):
    high = value.astype(BF16)
    low = (value - high.astype(F32)).astype(BF16)
    return high, low


def splat_kernel(
    nt,
    nd,
    cap,
    features,
    geometry,
    picked,
    tile_ids,
    tile_lists,
    live_counts,
    cotangent,
    image_out,
    grad_rx,
    ggeo_rx,
    own_feat,
    own_geo,
    feat_tx,
    feat_rx,
    feat_list,
    geo_rows,
    geo_tx,
    geo_rx,
    lists_rx,
    inv_vec,
    lists_sm,
    inv_sm,
    geo_part,
    geo,
    cot,
    place_mat,
    ahead_mat,
    behind_mat,
    fall,
    chain,
    later,
    weights,
    sums,
    light,
    carry,
    offs,
    grad_sum,
    grad_list,
    grad_tx,
    moment,
    ggeo_list,
    ggeo_tx,
    image_part,
    image_rx,
    local_sem,
    geo_sem,
    feat_sem,
    grad_sem,
    ggeo_sem,
    lists_send,
    lists_recv,
    light_send,
    light_recv,
    carry_send,
    carry_recv,
    image_send,
    image_recv,
):
    me = lax.axis_index("tile")
    my = lax.axis_index("depth")
    slots = nt * cap
    near = my + 1 - 2 * (my % 2)
    far = nd - 1 - my

    def greet(i, c):
        pl.semaphore_signal(
            barrier, inc=1, device_id={"tile": lax.rem(me + i, nt)}, device_id_type=MESH
        )
        return c

    barrier = pltpu.get_barrier_semaphore()
    lax.fori_loop(1, nt, greet, 0)
    for step in range(1, nd):
        pl.semaphore_signal(
            barrier, inc=1, device_id={"depth": lax.rem(my + step, nd)}, device_id_type=MESH
        )

    fetch_geo = pltpu.make_async_copy(geometry, own_geo, local_sem.at[0])
    fetch_geo.start()
    fetch_feat = pltpu.make_async_copy(
        features.at[:, pl.ds(pl.multiple_of(my * 32, 32), 32), :], own_feat, local_sem.at[1]
    )
    fetch_feat.start()
    fetch_cot = []
    for par in range(2):
        for ph in range(2):
            for high in range(2):
                copy = pltpu.make_async_copy(
                    cotangent.at[high * 2 + par, pl.ds(ph * 128, 128), :],
                    cot.at[par * 2 + ph, pl.ds(high * 128, 128), :],
                    local_sem.at[5 + par * 4 + ph * 2 + high],
                )
                copy.start()
                fetch_cot.append(copy)

    lane8 = iota((8, 128), 1)
    listed = jnp.zeros((8, 128), I32)
    for u in range(4):
        for g in range(2):
            for k in range(8):
                listed = jnp.where(lane8 == u * 16 + g * 8 + k, tile_lists[u, g, k], listed)
            listed = jnp.where(lane8 == 64 + u * 2 + g, live_counts[g, u], listed)
    lists_rx[my] = listed

    fetch_geo.wait()
    lane_group = iota((slots, 128), 1) // 32
    for r in range(2):
        total = jnp.zeros((slots, 128), F32)
        for m in range(4 if r == 0 else 2):
            shift = lax.rem(32 * m + 128 - 32 * my, 128)
            total = jnp.where(lane_group == m, pltpu.roll(own_geo[4 * r + m], shift, 1), total)
        geo_rows[r] = total

    def pick_geo(t, c):
        for j in range(cap):
            at = picked[j, t]
            first = geo_rows[0, pl.ds(at, 1), :]
            second = geo_rows[1, pl.ds(at, 1), :]
            geo_tx[t * cap + j] = jnp.concatenate([first, second], axis=0)
        return c

    lax.fori_loop(0, nt, pick_geo, 0, unroll=4)
    mine = pl.multiple_of(me * cap, cap)
    geo_rx[pl.ds(mine, cap)] = geo_tx[pl.ds(mine, cap)]

    def across_depth(source, target, send, recv, peer):
        return pltpu.make_async_remote_copy(
            src_ref=source,
            dst_ref=target,
            send_sem=send,
            recv_sem=recv,
            device_id={"depth": peer},
            device_id_type=MESH,
        )

    def scatter_tiles(source, target, sem):
        def send(i, c):
            peer = lax.rem(me + i, nt)
            there = pl.multiple_of(peer * cap, cap)
            pltpu.make_async_remote_copy(
                src_ref=source.at[pl.ds(there, cap)],
                dst_ref=target.at[pl.ds(mine, cap)],
                send_sem=sem.at[0],
                recv_sem=sem.at[1],
                device_id={"tile": peer},
                device_id_type=MESH,
            ).start()
            return c

        lax.fori_loop(1, nt, send, 0)

    def all_tiles(source, target, sem):
        many = (nt - 1) * cap
        return pltpu.make_async_remote_copy(
            src_ref=source.at[pl.ds(0, many)],
            dst_ref=target.at[pl.ds(0, many)],
            send_sem=sem.at[0],
            recv_sem=sem.at[1],
            device_id={"tile": lax.rem(me + 1, nt)},
            device_id_type=MESH,
        )

    pl.semaphore_wait(barrier, nt - 1 + nd - 1)
    for step in range(1, nd):
        peer = lax.rem(my + step, nd)
        across_depth(
            lists_rx.at[my], lists_rx.at[my], lists_send.at[peer], lists_recv.at[my], peer
        ).start()
    scatter_tiles(geo_tx, geo_rx, geo_sem)

    fetch_feat.wait()

    def pick_feat(t, c):
        for j in range(cap):
            feat_tx[t * cap + j] = own_feat[picked[j, t]]
        return c

    lax.fori_loop(0, nt, pick_feat, 0, unroll=4)
    feat_rx[pl.ds(mine, cap)] = feat_tx[pl.ds(mine, cap)]
    scatter_tiles(feat_tx, feat_rx, feat_sem)

    row_in = iota((256, 128), 0) % 128
    lane_out = iota((256, 128), 1)
    same_block = row_in // 32 == lane_out // 32
    before_mat = ones_where(same_block & (row_in < lane_out))
    after_mat = ones_where(same_block & (row_in > lane_out))
    place_key = lane_out - row_in // 32
    in_entry = iota((64, 256), 0)
    out_entry = iota((64, 256), 1) // 32

    def build(g, c):
        for h in range(2):
            place_mat[g * 2 + h] = ones_where(place_key == g * 8 + h * 4)
        want = out_entry + g * 8
        equal = ones_where(in_entry == want)
        less = ones_where(in_entry < want)
        more = ones_where(in_entry > want)
        ahead_mat[g] = jnp.concatenate([less, equal, less, equal], axis=0)
        behind_mat[g] = jnp.concatenate([more, equal, more, equal], axis=0)
        return c

    lax.fori_loop(0, 8, build, 0)

    for step in range(1, nd):
        other = lax.rem(my + step, nd)
        across_depth(
            lists_rx.at[other], lists_rx.at[other], lists_send.at[other], lists_recv.at[other], other
        ).wait_recv()
    to_scalar = pltpu.make_async_copy(lists_rx, lists_sm, local_sem.at[2])
    to_scalar.start()
    slot_of_row = iota((128, 128), 0)
    lane = iota((128, 128), 1)
    found = jnp.zeros((128, 128), I32)
    for q in range(nd):
        row = jnp.broadcast_to(lists_rx[q, 0:1, :], (128, 128))
        hit = (row == slot_of_row) & (lane < 32)
        found = found + jnp.where(hit, lane + 32 * q, 0)
    for shift in (64, 32, 16, 8, 4, 2, 1):
        found = found + pltpu.roll(found, shift, 1)
    inv_vec[...] = jnp.transpose(found)[0:8]
    to_scalar.wait()
    inv_copy = pltpu.make_async_copy(inv_vec, inv_sm, local_sem.at[3])
    inv_copy.start()

    def within(index):
        return jnp.clip(index, 0, slots - 1)

    def slot_at(par, g, k):
        return within(lists_sm[g // 2, 0, par * 16 + (g % 2) * 8 + k])

    def live_at(tile, g):
        return lists_sm[g // 2, 0, 64 + tile * 2 + g % 2]

    all_tiles(geo_tx, geo_rx, geo_sem).wait_recv()

    def sort_geo(at, c):
        for k in range(8):
            rows = geo_rx[slot_at(at // 8, at % 8, k)]
            group = at * 2 + k // 4
            for r in range(2):
                geo_part[r, k % 4, pl.ds(group, 1), :] = rows[r : r + 1, :]
        return c

    lax.fori_loop(0, 16, sort_geo, 0)
    lane_part = iota((32, 128), 1) // 32
    for p in range(6):
        r, m = p // 4, p % 4
        total = jnp.zeros((32, 128), F32)
        for i in range(4):
            shift = (32 * (i - m)) % 128
            part = geo_part[r, i]
            moved = pltpu.roll(part, shift, 1) if shift else part
            total = jnp.where(lane_part == i, moved, total)
        geo[p] = total

    column = iota((16, 128), 0).astype(F32) + 0.5
    entry_lane = iota((16, 128), 1) // 32
    left = iota((128, 128), 1) < 64

    def row_of(p, group):
        return jnp.broadcast_to(geo[p, pl.ds(group, 1), :], (16, 128))

    def origin(tile):
        return 16.0 * tile_ids[tile].astype(F32)

    def start_near(buffer, send, recv, chunk):
        whole = sums[...]
        buffer[chunk, 0] = jnp.where(left, whole[:128], pltpu.roll(whole[128:], 64, 1))
        across_depth(
            buffer.at[chunk, 0], buffer.at[chunk, 1], send.at[0, chunk], recv.at[0, chunk], near
        ).start()

    def start_far(buffer, send, recv, chunk):
        across_depth(
            buffer.at[chunk, 1], buffer.at[chunk, 1], send.at[0, chunk], recv.at[0, chunk], near
        ).wait_recv()
        buffer[chunk, 3] = buffer[chunk, 0] + buffer[chunk, 1]
        across_depth(
            buffer.at[chunk, 3], buffer.at[chunk, 2], send.at[1, chunk], recv.at[1, chunk], far
        ).start()

    def offsets_from(buffer, send, recv, chunk, use_near, use_far):
        across_depth(
            buffer.at[chunk, 2], buffer.at[chunk, 2], send.at[1, chunk], recv.at[1, chunk], far
        ).wait_recv()
        total = buffer[chunk, 3] + buffer[chunk, 2]
        same = use_near * buffer[chunk, 1] + use_far * buffer[chunk, 2]
        for high in range(2):
            if high == 0:
                both = jnp.where(left, total, pltpu.roll(same, 64, 1))
            else:
                both = jnp.where(left, pltpu.roll(total, 64, 1), same)
            top, rest = split_two(both)
            offs[pl.ds(high * 128, 128), :] = jnp.concatenate([top, rest], axis=1)

    odd = jnp.where(my % 2 == 1, 1.0, 0.0)
    upper = jnp.where(my >= 2, 1.0, 0.0)

    for chunk in range(4):
        par, ph = chunk // 2, chunk % 2
        sums[...] = jnp.zeros((256, 128), F32)

        def alpha_step(g, c, par=par, ph=ph, chunk=chunk):
            for h in range(2):
                group = (par * 8 + g) * 2 + h
                mean_x, mean_y = row_of(0, group), row_of(1, group)
                half_a = -0.5 * row_of(2, group)
                minus_b = -row_of(3, group)
                half_c = -0.5 * row_of(4, group)
                opacity = row_of(5, group)
                highs, lows = [], []
                for high in range(2):
                    tile = high * 2 + par
                    dx = column - (mean_x - origin(tile))
                    alive = entry_lane + h * 4 < live_at(tile, g)
                    ax = jnp.where(alive, half_a * dx * dx, -1e30)
                    for py in range(8):
                        dy = (py + ph * 8 + 0.5) - mean_y
                        power = dx * (minus_b * dy) + (ax + half_c * dy * dy)
                        falloff = jnp.exp(power)
                        fall[chunk, g * 2 + h, pl.ds(high * 128 + py * 16, 16), :] = falloff
                        top, rest = split_two(jnp.log(1.0 - opacity * falloff))
                        highs.append(top)
                        lows.append(rest)
                both = jnp.concatenate(
                    [jnp.concatenate(highs, axis=0), jnp.concatenate(lows, axis=0)], axis=1
                )
                right = jnp.concatenate([before_mat, place_mat[g * 2 + h]], axis=1)
                result = jnp.dot(both, right, preferred_element_type=F32)
                chain[chunk, g * 2 + h] = result[:, :128]
                sums[...] += result[:, 128:]
            return c

        lax.fori_loop(0, 8, alpha_step, 0)
        start_near(light, light_send, light_recv, chunk)
        if chunk:
            start_far(light, light_send, light_recv, chunk - 1)

    for copy in fetch_cot:
        copy.wait()
    inv_copy.wait()

    for chunk in range(4):
        par, ph = chunk // 2, chunk % 2
        if chunk == 1:
            start_far(light, light_send, light_recv, 3)
        offsets_from(light, light_send, light_recv, chunk, odd, upper)

        def weight_step(g, c, par=par, ph=ph, chunk=chunk):
            ahead = jnp.dot(offs[...], ahead_mat[g], preferred_element_type=F32)
            halves = []
            for h in range(2):
                group = (par * 8 + g) * 2 + h
                opacity = jnp.broadcast_to(geo[5, pl.ds(group, 1), :], (256, 128))
                through = jnp.exp(chain[chunk, g * 2 + h] + ahead[:, h * 128 : (h + 1) * 128])
                chain[chunk, g * 2 + h] = through
                halves.append((through * (opacity * fall[chunk, g * 2 + h])).astype(BF16))
            weight = jnp.concatenate(halves, axis=1)
            weights[chunk, g] = weight
            grad = lax.dot_general(
                weight, cot[chunk], (((0,), (0,)), ((), ())), preferred_element_type=F32
            )
            if ph == 0:
                grad_sum[g] = grad
            else:
                grad = grad + grad_sum[g]
                at = (g // 2) * 4 + par * 2 + g % 2
                grad_list[pl.ds(pl.multiple_of(at * 8, 8), 8)] = grad.astype(BF16).reshape(
                    8, 32, 128
                )
            return c

        lax.fori_loop(0, 8, weight_step, 0)

    def back_feat(k, c):
        grad_tx[k] = grad_list[within(inv_sm[0, k])]
        return c

    lax.fori_loop(0, slots, back_feat, 0, unroll=8)
    keep_own = pltpu.make_async_copy(
        grad_tx.at[pl.ds(mine, cap)], grad_rx.at[pl.ds(mine, cap)], local_sem.at[4]
    )
    keep_own.start()
    scatter_tiles(grad_tx, grad_rx, grad_sem)
    all_tiles(feat_tx, feat_rx, feat_sem).wait_recv()

    def sort_feat(at, c):
        for k in range(8):
            feat_list[at, pl.ds(k * 32, 32), :] = feat_rx[slot_at(at // 8, at % 8, k)]
        return c

    lax.fori_loop(0, 16, sort_feat, 0)
    image_part[...] = jnp.zeros(image_part.shape, F32)

    for chunk in range(4):
        par, ph = chunk // 2, chunk % 2
        sums[...] = jnp.zeros((256, 128), F32)

        def carry_step(g, c, par=par, ph=ph, chunk=chunk):
            feat = feat_list[par * 8 + g]
            shown = jnp.dot(weights[chunk, g], feat, preferred_element_type=F32)
            image_part[par, ph] += shown.reshape(2, 128, 128)
            dots = lax.dot_general(
                cot[chunk], feat, (((1,), (1,)), ((), ())), preferred_element_type=F32
            )
            for h in range(2):
                group = (par * 8 + g) * 2 + h
                opacity = jnp.broadcast_to(geo[5, pl.ds(group, 1), :], (256, 128))
                direct = dots[:, h * 128 : (h + 1) * 128] * chain[chunk, g * 2 + h]
                chain[chunk, g * 2 + h] = direct
                top, rest = split_two(direct * (opacity * fall[chunk, g * 2 + h]))
                both = jnp.concatenate([top, rest], axis=1)
                right = jnp.concatenate([after_mat, place_mat[g * 2 + h]], axis=1)
                result = jnp.dot(both, right, preferred_element_type=F32)
                later[chunk, g * 2 + h] = result[:, :128]
                sums[...] += result[:, 128:]
            return c

        lax.fori_loop(0, 8, carry_step, 0)
        start_near(carry, carry_send, carry_recv, chunk)
        if chunk:
            start_far(carry, carry_send, carry_recv, chunk - 1)

    for chunk in range(4):
        par, ph = chunk // 2, chunk % 2
        if chunk == 1:
            start_far(carry, carry_send, carry_recv, 3)
            for step in range(1, nd):
                peer = lax.rem(my + step, nd)
                across_depth(
                    image_part.at[
                        :, peer // 2, :, pl.ds(pl.multiple_of((peer % 2) * 64, 64), 64), :
                    ],
                    image_rx.at[my],
                    image_send.at[peer],
                    image_recv.at[my],
                    peer,
                ).start()
        offsets_from(carry, carry_send, carry_recv, chunk, 1.0 - odd, 1.0 - upper)

        def shape_step(g, c, par=par, ph=ph, chunk=chunk):
            behind = jnp.dot(offs[...], behind_mat[g], preferred_element_type=F32)
            for h in range(2):
                group = (par * 8 + g) * 2 + h
                mean_x, mean_y = row_of(0, group), row_of(1, group)
                opacity = row_of(5, group)
                parts = [jnp.zeros((16, 128), F32) for _ in range(6)]
                for high in range(2):
                    tile = high * 2 + par
                    dx = column - (mean_x - origin(tile))
                    flat = jnp.zeros((16, 128), F32)
                    tilt = jnp.zeros((16, 128), F32)
                    bend = jnp.zeros((16, 128), F32)
                    for py in range(8):
                        at = high * 128 + py * 16
                        rows = pl.ds(at, 16)
                        dy = (py + ph * 8 + 0.5) - mean_y
                        falloff = fall[chunk, g * 2 + h, rows, :]
                        after = (
                            later[chunk, g * 2 + h, rows, :]
                            + behind[at : at + 16, h * 128 : (h + 1) * 128]
                        )
                        alpha_grad = chain[chunk, g * 2 + h, rows, :] - after / (
                            1.0 - opacity * falloff
                        )
                        term = alpha_grad * falloff
                        term_y = term * dy
                        flat = flat + term
                        tilt = tilt + term_y
                        bend = bend + term_y * dy
                    flat_x = flat * dx
                    adds = [flat, flat_x, tilt, flat_x * dx, tilt * dx, bend]
                    parts = [a + b for a, b in zip(parts, adds)]
                for i, part in enumerate(parts):
                    folded = jnp.sum(part, axis=0, keepdims=True)
                    if ph:
                        folded = folded + moment[i, pl.ds(group, 1), :]
                    moment[i, pl.ds(group, 1), :] = folded
            return c

        lax.fori_loop(0, 8, shape_step, 0)

    one, sx, sy, sxx, sxy, syy = [moment[i] for i in range(6)]
    conic_a, conic_b, conic_c, opac = [geo[p] for p in (2, 3, 4, 5)]
    ggeo = [
        opac * (conic_a * sx + conic_b * sy),
        opac * (conic_b * sx + conic_c * sy),
        -0.5 * opac * sxx,
        -opac * sxy,
        -0.5 * opac * syy,
        one,
    ]
    for i in range(4):
        for r in range(2):
            total = jnp.zeros((32, 128), F32)
            for m in range(4 if r == 0 else 2):
                shift = (32 * (m - i)) % 128
                part = ggeo[4 * r + m]
                moved = pltpu.roll(part, shift, 1) if shift else part
                total = jnp.where(lane_part == m, moved, total)
            ggeo_list[r, i] = total

    def back_geo(k, c):
        at = within(inv_sm[0, k])
        g = (at // 32) * 2 + (at // 8) % 2
        group = (((at // 16) % 2) * 8 + g) * 2 + (at % 8) // 4
        first = ggeo_list[0, at % 4, pl.ds(group, 1), :]
        second = ggeo_list[1, at % 4, pl.ds(group, 1), :]
        ggeo_tx[k] = jnp.concatenate([first, second], axis=0)
        return c

    lax.fori_loop(0, slots, back_geo, 0, unroll=8)
    keep_geo = pltpu.make_async_copy(
        ggeo_tx.at[pl.ds(mine, cap)], ggeo_rx.at[pl.ds(mine, cap)], local_sem.at[13]
    )
    keep_geo.start()
    scatter_tiles(ggeo_tx, ggeo_rx, ggeo_sem)

    image = image_part[:, my // 2, :, pl.ds(pl.multiple_of((my % 2) * 64, 64), 64), :]
    for step in range(1, nd):
        other = lax.rem(my + step, nd)
        across_depth(
            image_rx.at[other], image_rx.at[other], image_send.at[other], image_recv.at[other], other
        ).wait_recv()
        image = image + image_rx[other]
    for par in range(2):
        for high in range(2):
            image_out[high * 2 + par] = image[par, high].astype(BF16)

    for step in range(1, nd):
        other = lax.rem(my + step, nd)
        across_depth(
            lists_rx.at[other], lists_rx.at[other], lists_send.at[other], lists_recv.at[other], other
        ).wait_send()
        across_depth(
            image_rx.at[other], image_rx.at[other], image_send.at[other], image_recv.at[other], other
        ).wait_send()
    for buffer, send, recv in ((light, light_send, light_recv), (carry, carry_send, carry_recv)):
        for chunk in range(4):
            across_depth(
                buffer.at[chunk, 0], buffer.at[chunk, 1], send.at[0, chunk], recv.at[0, chunk], near
            ).wait_send()
            across_depth(
                buffer.at[chunk, 3], buffer.at[chunk, 2], send.at[1, chunk], recv.at[1, chunk], far
            ).wait_send()
    all_tiles(geo_tx, geo_rx, geo_sem).wait_send()
    all_tiles(feat_tx, feat_rx, feat_sem).wait_send()
    keep_own.wait()
    keep_geo.wait()
    all_tiles(grad_tx, grad_rx, grad_sem).wait()
    all_tiles(ggeo_tx, ggeo_rx, ggeo_sem).wait()


def owner_kernel(picked, grad_rx, ggeo_rx, grad_out, ggeo_out, rows):
    cap, nt = picked.shape

    def put(t, c):
        for j in range(cap):
            k = t * cap + j
            at = picked[j, t]
            grad_out[at] = grad_rx[k].astype(F32)
            for r in range(2):
                rows[r, pl.ds(at, 1), :] = ggeo_rx[k, r : r + 1, :]
        return c

    lax.fori_loop(0, nt, put, 0, unroll=4)
    for r in range(2):
        turned = jnp.transpose(rows[r])
        for m in range(4 if r == 0 else 2):
            ggeo_out[4 * r + m] = turned[m * 32 : m * 32 + 32]


def local(features, geometry, send_lists, tile_ids, tile_lists, live_counts, cotangent):
    nt, nd = lax.axis_size("tile"), lax.axis_size("depth")
    cap = send_lists.shape[2]
    slots = nt * cap
    blocks = features.shape[0]
    picked = jnp.transpose(send_lists[0])

    vmem = pl.BlockSpec(memory_space=pltpu.VMEM)
    smem = pl.BlockSpec(memory_space=pltpu.SMEM)
    hbm = pl.BlockSpec(memory_space=pl.ANY)
    dma = pltpu.SemaphoreType.DMA
    big = pltpu.VMEM((4, 16, 256, 128), F32)
    image_out, grad_rx, ggeo_rx = pl.pallas_call(
        functools.partial(splat_kernel, nt, nd, cap),
        out_shape=(
            jax.ShapeDtypeStruct((4, 64, 128), BF16),
            jax.ShapeDtypeStruct((slots, 32, 128), BF16),
            jax.ShapeDtypeStruct((slots, 2, 128), F32),
        ),
        in_specs=[hbm, hbm, smem, smem, smem, smem, hbm],
        out_specs=(vmem, hbm, hbm),
        scratch_shapes=[
            pltpu.VMEM((blocks, 32, 128), BF16),
            pltpu.VMEM((6, blocks, 128), F32),
            pltpu.VMEM((slots, 32, 128), BF16),
            pltpu.VMEM((slots, 32, 128), BF16),
            pltpu.VMEM((16, 256, 128), BF16),
            pltpu.VMEM((2, blocks, 128), F32),
            pltpu.VMEM((slots, 2, 128), F32),
            pltpu.VMEM((slots, 2, 128), F32),
            pltpu.VMEM((nd, 8, 128), I32),
            pltpu.VMEM((8, 128), I32),
            pltpu.SMEM((nd, 8, 128), I32),
            pltpu.SMEM((8, 128), I32),
            pltpu.VMEM((2, 4, 32, 128), F32),
            pltpu.VMEM((6, 32, 128), F32),
            pltpu.VMEM((4, 256, 128), BF16),
            pltpu.VMEM((16, 256, 128), BF16),
            pltpu.VMEM((8, 256, 256), BF16),
            pltpu.VMEM((8, 256, 256), BF16),
            big,
            big,
            big,
            pltpu.VMEM((4, 8, 256, 256), BF16),
            pltpu.VMEM((256, 128), F32),
            pltpu.VMEM((4, 4, 128, 128), F32),
            pltpu.VMEM((4, 4, 128, 128), F32),
            pltpu.VMEM((256, 256), BF16),
            pltpu.VMEM((8, 256, 128), F32),
            pltpu.VMEM((slots, 32, 128), BF16),
            pltpu.VMEM((slots, 32, 128), BF16),
            pltpu.VMEM((6, 32, 128), F32),
            pltpu.VMEM((2, 4, 32, 128), F32),
            pltpu.VMEM((slots, 2, 128), F32),
            pltpu.VMEM((2, 2, 2, 128, 128), F32),
            pltpu.VMEM((nd, 2, 2, 64, 128), F32),
            dma((14,)),
            dma((2,)),
            dma((2,)),
            dma((2,)),
            dma((2,)),
            dma((nd,)),
            dma((nd,)),
            dma((2, 4)),
            dma((2, 4)),
            dma((2, 4)),
            dma((2, 4)),
            dma((nd,)),
            dma((nd,)),
        ],
        compiler_params=pltpu.CompilerParams(
            collective_id=0, has_side_effects=True, vmem_limit_bytes=62 * 1024 * 1024
        ),
        name="splat",
    )(
        features,
        jnp.transpose(geometry, (1, 0, 2)),
        picked,
        tile_ids,
        tile_lists,
        jnp.transpose(live_counts),
        cotangent,
    )

    feature_grads, geometry_grads = pl.pallas_call(
        owner_kernel,
        out_shape=(
            jax.ShapeDtypeStruct((blocks, 32, 128), F32),
            jax.ShapeDtypeStruct((6, 32, blocks), F32),
        ),
        in_specs=[smem, vmem, vmem],
        out_specs=(vmem, vmem),
        scratch_shapes=[pltpu.VMEM((2, blocks, 128), F32)],
        name="owner",
    )(picked, grad_rx, ggeo_rx)
    return image_out, feature_grads, jnp.transpose(geometry_grads, (2, 0, 1))


def solution(mesh):
    placed = (
        P("tile", None, None),
        P("tile", None, None),
        P("tile", None, None),
        P("tile"),
        P("tile", "depth", None),
        P("tile", "depth"),
        P("tile", None, None),
    )
    return jax.shard_map(
        local,
        mesh=mesh,
        in_specs=placed,
        out_specs=(P("tile", "depth", None), P("tile", "depth", None), P("tile", None, "depth")),
        check_vma=False,
    )
```

```python
import functools

import jax
import jax.numpy as jnp
from jax import lax
from jax.experimental import pallas as pl
from jax.experimental.pallas import tpu as pltpu
from jax.sharding import PartitionSpec as P

MESH = pl.DeviceIdType.MESH
F32 = jnp.float32
BF16 = jnp.bfloat16
I32 = jnp.int32


def iota(shape, dim):
    return lax.broadcasted_iota(I32, shape, dim)


def ones_where(mask):
    return jnp.where(mask, 1.0, 0.0).astype(BF16)


def split_two(value):
    high = value.astype(BF16)
    low = (value - high.astype(F32)).astype(BF16)
    return high, low


def group_of(par, g, h):
    return (g // 2) * 8 + par * 4 + (g % 2) * 2 + h


def paired(step):
    def both(i, c):
        step(i * 2, c)
        step(i * 2 + 1, c)
        return c

    return both


def splat_kernel(
    nt,
    nd,
    cap,
    features,
    geometry,
    picked,
    tile_ids,
    tile_lists,
    live_counts,
    cotangent,
    image_out,
    grad_rx,
    ggeo_rx,
    own_feat,
    own_geo,
    feat_tx,
    feat_rx,
    feat_list,
    geo_rows,
    geo_tx,
    geo_rx,
    lists_rx,
    inv_vec,
    lists_sm,
    inv_sm,
    geo_part,
    geo,
    cot,
    cot_turned,
    place_mat,
    ahead_mat,
    behind_mat,
    fall,
    chain,
    thru,
    later,
    weights,
    sums,
    light,
    carry,
    offs,
    grad_sum,
    grad_list,
    grad_tx,
    moment,
    ggeo_list,
    ggeo_tx,
    image_part,
    image_rx,
    local_sem,
    geo_sem,
    feat_sem,
    grad_sem,
    ggeo_sem,
    lists_send,
    lists_recv,
    light_send,
    light_recv,
    carry_send,
    carry_recv,
    image_send,
    image_recv,
):
    me = lax.axis_index("tile")
    my = lax.axis_index("depth")
    slots = nt * cap
    near = my + 1 - 2 * (my % 2)
    far = nd - 1 - my

    def greet(i, c):
        pl.semaphore_signal(
            barrier, inc=1, device_id={"tile": lax.rem(me + i, nt)}, device_id_type=MESH
        )
        return c

    barrier = pltpu.get_barrier_semaphore()
    lax.fori_loop(1, nt, greet, 0)
    for step in range(1, nd):
        pl.semaphore_signal(
            barrier, inc=1, device_id={"depth": lax.rem(my + step, nd)}, device_id_type=MESH
        )

    fetch_geo = pltpu.make_async_copy(geometry, own_geo, local_sem.at[0])
    fetch_geo.start()
    fetch_feat = pltpu.make_async_copy(
        features.at[:, pl.ds(pl.multiple_of(my * 32, 32), 32), :], own_feat, local_sem.at[1]
    )
    fetch_feat.start()
    fetch_cot = []
    for par in range(2):
        for ph in range(2):
            for high in range(2):
                copy = pltpu.make_async_copy(
                    cotangent.at[high * 2 + par, pl.ds(ph * 128, 128), :],
                    cot.at[par * 2 + ph, pl.ds(high * 128, 128), :],
                    local_sem.at[5 + par * 4 + ph * 2 + high],
                )
                copy.start()
                fetch_cot.append(copy)

    lane8 = iota((8, 128), 1)
    listed = jnp.zeros((8, 128), I32)
    for u in range(4):
        for g in range(2):
            for k in range(8):
                listed = jnp.where(lane8 == u * 16 + g * 8 + k, tile_lists[u, g, k], listed)
            listed = jnp.where(lane8 == 64 + u * 2 + g, live_counts[g, u], listed)
    lists_rx[my] = listed

    fetch_geo.wait()
    lane_group = iota((slots, 128), 1) // 32
    for r in range(2):
        total = jnp.zeros((slots, 128), F32)
        for m in range(4 if r == 0 else 2):
            shift = lax.rem(32 * m + 128 - 32 * my, 128)
            total = jnp.where(lane_group == m, pltpu.roll(own_geo[4 * r + m], shift, 1), total)
        geo_rows[r] = total

    def pick_geo(t, c):
        for j in range(cap):
            at = picked[j, t]
            first = geo_rows[0, pl.ds(at, 1), :]
            second = geo_rows[1, pl.ds(at, 1), :]
            geo_tx[t * cap + j] = jnp.concatenate([first, second], axis=0)
        return c

    lax.fori_loop(0, nt, pick_geo, 0, unroll=4)
    mine = pl.multiple_of(me * cap, cap)
    geo_rx[pl.ds(mine, cap)] = geo_tx[pl.ds(mine, cap)]

    def across_depth(source, target, send, recv, peer):
        return pltpu.make_async_remote_copy(
            src_ref=source,
            dst_ref=target,
            send_sem=send,
            recv_sem=recv,
            device_id={"depth": peer},
            device_id_type=MESH,
        )

    def scatter_tiles(source, target, sem):
        def send(i, c):
            peer = lax.rem(me + i, nt)
            there = pl.multiple_of(peer * cap, cap)
            pltpu.make_async_remote_copy(
                src_ref=source.at[pl.ds(there, cap)],
                dst_ref=target.at[pl.ds(mine, cap)],
                send_sem=sem.at[0],
                recv_sem=sem.at[1],
                device_id={"tile": peer},
                device_id_type=MESH,
            ).start()
            return c

        lax.fori_loop(1, nt, send, 0)

    def all_tiles(source, target, sem):
        many = (nt - 1) * cap
        return pltpu.make_async_remote_copy(
            src_ref=source.at[pl.ds(0, many)],
            dst_ref=target.at[pl.ds(0, many)],
            send_sem=sem.at[0],
            recv_sem=sem.at[1],
            device_id={"tile": lax.rem(me + 1, nt)},
            device_id_type=MESH,
        )

    fetch_feat.wait()

    def pick_feat(t, c):
        for j in range(cap):
            feat_tx[t * cap + j] = own_feat[picked[j, t]]
        return c

    lax.fori_loop(0, nt, pick_feat, 0, unroll=4)
    feat_rx[pl.ds(mine, cap)] = feat_tx[pl.ds(mine, cap)]

    row_in = iota((256, 128), 0) % 128
    lane_out = iota((256, 128), 1)
    same_block = row_in // 32 == lane_out // 32
    before_mat = ones_where(same_block & (row_in < lane_out))
    after_mat = ones_where(same_block & (row_in > lane_out))
    place_key = lane_out - row_in // 32
    in_entry = iota((64, 256), 0)
    out_entry = iota((64, 256), 1) // 32

    def build(g, c):
        for h in range(2):
            place_mat[g * 2 + h] = ones_where(place_key == g * 8 + h * 4)
        want = out_entry + g * 8
        equal = ones_where(in_entry == want)
        less = ones_where(in_entry < want)
        more = ones_where(in_entry > want)
        ahead_mat[g] = jnp.concatenate([less, equal, less, equal], axis=0)
        behind_mat[g] = jnp.concatenate([more, equal, more, equal], axis=0)
        return c

    lax.fori_loop(0, 8, build, 0)

    for copy in fetch_cot:
        copy.wait()
    for chunk in range(4):
        cot_turned[chunk] = jnp.transpose(cot[chunk].astype(F32)).astype(BF16)

    pl.semaphore_wait(barrier, nt - 1 + nd - 1)
    for step in range(1, nd):
        peer = lax.rem(my + step, nd)
        across_depth(
            lists_rx.at[my], lists_rx.at[my], lists_send.at[peer], lists_recv.at[my], peer
        ).start()
    scatter_tiles(geo_tx, geo_rx, geo_sem)
    scatter_tiles(feat_tx, feat_rx, feat_sem)

    for step in range(1, nd):
        other = lax.rem(my + step, nd)
        across_depth(
            lists_rx.at[other], lists_rx.at[other], lists_send.at[other], lists_recv.at[other], other
        ).wait_recv()
    to_scalar = pltpu.make_async_copy(lists_rx, lists_sm, local_sem.at[2])
    to_scalar.start()
    slot_of_row = iota((128, 128), 0)
    lane = iota((128, 128), 1)
    found = jnp.zeros((128, 128), I32)
    for q in range(nd):
        row = jnp.broadcast_to(lists_rx[q, 0:1, :], (128, 128))
        hit = (row == slot_of_row) & (lane < 32)
        found = found + jnp.where(hit, lane + 32 * q, 0)
    for shift in (64, 32, 16, 8, 4, 2, 1):
        found = found + pltpu.roll(found, shift, 1)
    inv_vec[...] = jnp.transpose(found)[0:8]
    to_scalar.wait()
    inv_copy = pltpu.make_async_copy(inv_vec, inv_sm, local_sem.at[3])
    inv_copy.start()

    def within(index):
        return jnp.clip(index, 0, slots - 1)

    def slot_at(par, g, k):
        return within(lists_sm[g // 2, 0, par * 16 + (g % 2) * 8 + k])

    def live_at(tile, g):
        return lists_sm[g // 2, 0, 64 + tile * 2 + g % 2]

    all_tiles(geo_tx, geo_rx, geo_sem).wait_recv()

    def sort_geo(at, c):
        for k in range(8):
            rows = geo_rx[slot_at(at // 8, at % 8, k)]
            group = group_of(at // 8, at % 8, k // 4)
            for r in range(2):
                geo_part[r, k % 4, pl.ds(group, 1), :] = rows[r : r + 1, :]
        return c

    lax.fori_loop(0, 16, sort_geo, 0)
    lane_part = iota((32, 128), 1) // 32
    for p in range(6):
        r, m = p // 4, p % 4
        total = jnp.zeros((32, 128), F32)
        for i in range(4):
            shift = (32 * (i - m)) % 128
            part = geo_part[r, i]
            moved = pltpu.roll(part, shift, 1) if shift else part
            total = jnp.where(lane_part == i, moved, total)
        geo[p] = total

    column = iota((16, 128), 0).astype(F32) + 0.5
    entry_lane = iota((16, 128), 1) // 32
    left = iota((128, 128), 1) < 64

    def row_of(p, group):
        return jnp.broadcast_to(geo[p, pl.ds(group, 1), :], (16, 128))

    def origin(tile):
        return 16.0 * tile_ids[tile].astype(F32)

    def start_near(buffer, send, recv, chunk):
        whole = sums[...]
        buffer[chunk, 0] = jnp.where(left, whole[:128], pltpu.roll(whole[128:], 64, 1))
        across_depth(
            buffer.at[chunk, 0], buffer.at[chunk, 1], send.at[0, chunk], recv.at[0, chunk], near
        ).start()

    def start_far(buffer, send, recv, chunk):
        across_depth(
            buffer.at[chunk, 1], buffer.at[chunk, 1], send.at[0, chunk], recv.at[0, chunk], near
        ).wait_recv()
        buffer[chunk, 3] = buffer[chunk, 0] + buffer[chunk, 1]
        across_depth(
            buffer.at[chunk, 3], buffer.at[chunk, 2], send.at[1, chunk], recv.at[1, chunk], far
        ).start()

    def offsets_from(buffer, send, recv, chunk, use_near, use_far):
        across_depth(
            buffer.at[chunk, 2], buffer.at[chunk, 2], send.at[1, chunk], recv.at[1, chunk], far
        ).wait_recv()
        total = buffer[chunk, 3] + buffer[chunk, 2]
        same = use_near * buffer[chunk, 1] + use_far * buffer[chunk, 2]
        for high in range(2):
            if high == 0:
                both = jnp.where(left, total, pltpu.roll(same, 64, 1))
            else:
                both = jnp.where(left, pltpu.roll(total, 64, 1), same)
            top, rest = split_two(both)
            offs[pl.ds(high * 128, 128), :] = jnp.concatenate([top, rest], axis=1)

    odd = jnp.where(my % 2 == 1, 1.0, 0.0)
    upper = jnp.where(my >= 2, 1.0, 0.0)

    for chunk in range(4):
        par, ph = chunk // 2, chunk % 2
        sums[...] = jnp.zeros((256, 128), F32)

        def alpha_step(g, c, par=par, ph=ph, chunk=chunk):
            for h in range(2):
                group = group_of(par, g, h)
                mean_x, mean_y = row_of(0, group), row_of(1, group)
                half_a = -0.5 * row_of(2, group)
                minus_b = -row_of(3, group)
                half_c = -0.5 * row_of(4, group)
                opacity = row_of(5, group)
                highs, lows = [], []
                for high in range(2):
                    tile = high * 2 + par
                    dx = column - (mean_x - origin(tile))
                    alive = entry_lane + h * 4 < live_at(tile, g)
                    ax = jnp.where(alive, half_a * dx * dx, -1e30)
                    for py in range(8):
                        dy = (py + ph * 8 + 0.5) - mean_y
                        power = dx * (minus_b * dy) + (ax + half_c * dy * dy)
                        falloff = jnp.exp(power)
                        fall[chunk, g * 2 + h, pl.ds(high * 128 + py * 16, 16), :] = falloff
                        top, rest = split_two(jnp.log(1.0 - opacity * falloff))
                        highs.append(top)
                        lows.append(rest)
                both = jnp.concatenate(
                    [jnp.concatenate(highs, axis=0), jnp.concatenate(lows, axis=0)], axis=1
                )
                right = jnp.concatenate([before_mat, place_mat[g * 2 + h]], axis=1)
                result = jnp.dot(both, right, preferred_element_type=F32)
                chain[chunk, g * 2 + h] = result[:, :128]
                sums[...] += result[:, 128:]
            return c

        lax.fori_loop(0, 4, paired(alpha_step), 0)
        start_near(light, light_send, light_recv, chunk)
        if chunk:
            start_far(light, light_send, light_recv, chunk - 1)

    inv_copy.wait()

    for chunk in range(4):
        par, ph = chunk // 2, chunk % 2
        if chunk == 1:
            start_far(light, light_send, light_recv, 3)
        offsets_from(light, light_send, light_recv, chunk, odd, upper)

        def weight_step(g, c, par=par, ph=ph, chunk=chunk):
            ahead = jnp.dot(offs[...], ahead_mat[g], preferred_element_type=F32)
            halves = []
            for h in range(2):
                group = group_of(par, g, h)
                opacity = jnp.broadcast_to(geo[5, pl.ds(group, 1), :], (256, 128))
                through = jnp.exp(chain[chunk, g * 2 + h] + ahead[:, h * 128 : (h + 1) * 128])
                thru[chunk, g * 2 + h] = through
                halves.append((through * (opacity * fall[chunk, g * 2 + h])).astype(BF16))
            weight = jnp.concatenate(halves, axis=1)
            weights[chunk, g] = weight
            grad = jnp.dot(cot_turned[chunk], weight, preferred_element_type=F32)
            if ph == 0:
                grad_sum[g] = grad
            else:
                grad = grad + grad_sum[g]
                at = (g // 2) * 4 + par * 2 + g % 2
                grad_list[pl.ds(pl.multiple_of(at * 8, 8), 8)] = jnp.transpose(grad).astype(
                    BF16
                ).reshape(8, 32, 128)
            return c

        lax.fori_loop(0, 4, paired(weight_step), 0)

    def back_feat(k, c):
        grad_tx[k] = grad_list[within(inv_sm[0, k])]
        return c

    lax.fori_loop(0, slots, back_feat, 0, unroll=8)
    keep_own = pltpu.make_async_copy(
        grad_tx.at[pl.ds(mine, cap)], grad_rx.at[pl.ds(mine, cap)], local_sem.at[4]
    )
    keep_own.start()
    scatter_tiles(grad_tx, grad_rx, grad_sem)
    all_tiles(feat_tx, feat_rx, feat_sem).wait_recv()

    def sort_feat(at, c):
        for k in range(8):
            feat_list[at, pl.ds(k * 32, 32), :] = feat_rx[slot_at(at // 8, at % 8, k)]
        return c

    lax.fori_loop(0, 16, sort_feat, 0)
    image_part[...] = jnp.zeros(image_part.shape, F32)

    for chunk in range(4):
        par, ph = chunk // 2, chunk % 2
        sums[...] = jnp.zeros((256, 128), F32)

        def carry_step(g, c, par=par, ph=ph, chunk=chunk):
            feat = feat_list[par * 8 + g]
            shown = jnp.dot(weights[chunk, g], feat, preferred_element_type=F32)
            image_part[par, ph] += shown.reshape(2, 128, 128)
            dots = lax.dot_general(
                cot[chunk], feat, (((1,), (1,)), ((), ())), preferred_element_type=F32
            )
            for h in range(2):
                group = group_of(par, g, h)
                opacity = jnp.broadcast_to(geo[5, pl.ds(group, 1), :], (256, 128))
                direct = dots[:, h * 128 : (h + 1) * 128] * thru[chunk, g * 2 + h]
                chain[chunk, g * 2 + h] = direct
                top, rest = split_two(direct * (opacity * fall[chunk, g * 2 + h]))
                both = jnp.concatenate([top, rest], axis=1)
                right = jnp.concatenate([after_mat, place_mat[g * 2 + h]], axis=1)
                result = jnp.dot(both, right, preferred_element_type=F32)
                later[chunk, g * 2 + h] = result[:, :128]
                sums[...] += result[:, 128:]
            return c

        lax.fori_loop(0, 4, paired(carry_step), 0)
        start_near(carry, carry_send, carry_recv, chunk)
        if chunk:
            start_far(carry, carry_send, carry_recv, chunk - 1)

    for chunk in range(4):
        par, ph = chunk // 2, chunk % 2
        if chunk == 1:
            start_far(carry, carry_send, carry_recv, 3)
            for step in range(1, nd):
                peer = lax.rem(my + step, nd)
                across_depth(
                    image_part.at[
                        :, peer // 2, :, pl.ds(pl.multiple_of((peer % 2) * 64, 64), 64), :
                    ],
                    image_rx.at[my],
                    image_send.at[peer],
                    image_recv.at[my],
                    peer,
                ).start()
        offsets_from(carry, carry_send, carry_recv, chunk, 1.0 - odd, 1.0 - upper)

        def shape_step(g, c, par=par, ph=ph, chunk=chunk):
            behind = jnp.dot(offs[...], behind_mat[g], preferred_element_type=F32)
            for h in range(2):
                group = group_of(par, g, h)
                mean_x, mean_y = row_of(0, group), row_of(1, group)
                opacity = row_of(5, group)
                parts = [jnp.zeros((16, 128), F32) for _ in range(6)]
                for high in range(2):
                    tile = high * 2 + par
                    dx = column - (mean_x - origin(tile))
                    flat = jnp.zeros((16, 128), F32)
                    tilt = jnp.zeros((16, 128), F32)
                    bend = jnp.zeros((16, 128), F32)
                    for py in range(8):
                        at = high * 128 + py * 16
                        rows = pl.ds(at, 16)
                        dy = (py + ph * 8 + 0.5) - mean_y
                        falloff = fall[chunk, g * 2 + h, rows, :]
                        after = (
                            later[chunk, g * 2 + h, rows, :]
                            + behind[at : at + 16, h * 128 : (h + 1) * 128]
                        )
                        alpha_grad = chain[chunk, g * 2 + h, rows, :] - after / (
                            1.0 - opacity * falloff
                        )
                        term = alpha_grad * falloff
                        term_y = term * dy
                        flat = flat + term
                        tilt = tilt + term_y
                        bend = bend + term_y * dy
                    flat_x = flat * dx
                    adds = [flat, flat_x, tilt, flat_x * dx, tilt * dx, bend]
                    parts = [a + b for a, b in zip(parts, adds)]
                for i, part in enumerate(parts):
                    folded = jnp.sum(part, axis=0, keepdims=True)
                    if ph:
                        folded = folded + moment[i, pl.ds(group, 1), :]
                    moment[i, pl.ds(group, 1), :] = folded
            return c

        lax.fori_loop(0, 4, paired(shape_step), 0)

    one, sx, sy, sxx, sxy, syy = [moment[i] for i in range(6)]
    conic_a, conic_b, conic_c, opac = [geo[p] for p in (2, 3, 4, 5)]
    ggeo = [
        opac * (conic_a * sx + conic_b * sy),
        opac * (conic_b * sx + conic_c * sy),
        -0.5 * opac * sxx,
        -opac * sxy,
        -0.5 * opac * syy,
        one,
    ]
    for i in range(4):
        for r in range(2):
            total = jnp.zeros((32, 128), F32)
            for m in range(4 if r == 0 else 2):
                shift = (32 * (m - i)) % 128
                part = ggeo[4 * r + m]
                moved = pltpu.roll(part, shift, 1) if shift else part
                total = jnp.where(lane_part == m, moved, total)
            for group in range(32):
                ggeo_list[group * 4 + i, r : r + 1, :] = total[group : group + 1]

    def back_geo(k, c):
        ggeo_tx[k] = ggeo_list[within(inv_sm[0, k])]
        return c

    lax.fori_loop(0, slots, back_geo, 0, unroll=8)
    keep_geo = pltpu.make_async_copy(
        ggeo_tx.at[pl.ds(mine, cap)], ggeo_rx.at[pl.ds(mine, cap)], local_sem.at[13]
    )
    keep_geo.start()
    scatter_tiles(ggeo_tx, ggeo_rx, ggeo_sem)

    image = image_part[:, my // 2, :, pl.ds(pl.multiple_of((my % 2) * 64, 64), 64), :]
    for step in range(1, nd):
        other = lax.rem(my + step, nd)
        across_depth(
            image_rx.at[other], image_rx.at[other], image_send.at[other], image_recv.at[other], other
        ).wait_recv()
        image = image + image_rx[other]
    for par in range(2):
        for high in range(2):
            image_out[high * 2 + par] = image[par, high].astype(BF16)

    for step in range(1, nd):
        other = lax.rem(my + step, nd)
        across_depth(
            lists_rx.at[other], lists_rx.at[other], lists_send.at[other], lists_recv.at[other], other
        ).wait_send()
        across_depth(
            image_rx.at[other], image_rx.at[other], image_send.at[other], image_recv.at[other], other
        ).wait_send()
    for buffer, send, recv in ((light, light_send, light_recv), (carry, carry_send, carry_recv)):
        for chunk in range(4):
            across_depth(
                buffer.at[chunk, 0], buffer.at[chunk, 1], send.at[0, chunk], recv.at[0, chunk], near
            ).wait_send()
            across_depth(
                buffer.at[chunk, 3], buffer.at[chunk, 2], send.at[1, chunk], recv.at[1, chunk], far
            ).wait_send()
    all_tiles(geo_tx, geo_rx, geo_sem).wait_send()
    all_tiles(feat_tx, feat_rx, feat_sem).wait_send()
    keep_own.wait()
    keep_geo.wait()
    all_tiles(grad_tx, grad_rx, grad_sem).wait()
    all_tiles(ggeo_tx, ggeo_rx, ggeo_sem).wait()


def owner_kernel(picked, grad_rx, ggeo_rx, image, grad_out, ggeo_out, image_out, rows):
    cap, nt = picked.shape
    image_out[...] = image[...]

    def put(t, c):
        for j in range(cap):
            k = t * cap + j
            at = picked[j, t]
            grad_out[at] = grad_rx[k].astype(F32)
            for r in range(2):
                rows[r, pl.ds(at, 1), :] = ggeo_rx[k, r : r + 1, :]
        return c

    lax.fori_loop(0, nt, put, 0, unroll=4)
    for r in range(2):
        turned = jnp.transpose(rows[r])
        for m in range(4 if r == 0 else 2):
            ggeo_out[4 * r + m] = turned[m * 32 : m * 32 + 32]


def local(features, geometry, send_lists, tile_ids, tile_lists, live_counts, cotangent):
    nt, nd = lax.axis_size("tile"), lax.axis_size("depth")
    cap = send_lists.shape[2]
    slots = nt * cap
    blocks = features.shape[0]
    picked = jnp.transpose(send_lists[0])

    vmem = pl.BlockSpec(memory_space=pltpu.VMEM)
    smem = pl.BlockSpec(memory_space=pltpu.SMEM)
    hbm = pl.BlockSpec(memory_space=pl.ANY)
    dma = pltpu.SemaphoreType.DMA
    big = pltpu.VMEM((4, 16, 256, 128), F32)
    image, grad_rx, ggeo_rx = pl.pallas_call(
        functools.partial(splat_kernel, nt, nd, cap),
        out_shape=(
            jax.ShapeDtypeStruct((4, 64, 128), BF16),
            jax.ShapeDtypeStruct((slots, 32, 128), BF16),
            jax.ShapeDtypeStruct((slots, 2, 128), F32),
        ),
        in_specs=[hbm, hbm, smem, smem, smem, smem, hbm],
        out_specs=(vmem, hbm, hbm),
        scratch_shapes=[
            pltpu.VMEM((blocks, 32, 128), BF16),
            pltpu.VMEM((6, blocks, 128), F32),
            pltpu.VMEM((slots, 32, 128), BF16),
            pltpu.VMEM((slots, 32, 128), BF16),
            pltpu.VMEM((16, 256, 128), BF16),
            pltpu.VMEM((2, blocks, 128), F32),
            pltpu.VMEM((slots, 2, 128), F32),
            pltpu.VMEM((slots, 2, 128), F32),
            pltpu.VMEM((nd, 8, 128), I32),
            pltpu.VMEM((8, 128), I32),
            pltpu.SMEM((nd, 8, 128), I32),
            pltpu.SMEM((8, 128), I32),
            pltpu.VMEM((2, 4, 32, 128), F32),
            pltpu.VMEM((6, 32, 128), F32),
            pltpu.VMEM((4, 256, 128), BF16),
            pltpu.VMEM((4, 128, 256), BF16),
            pltpu.VMEM((16, 256, 128), BF16),
            pltpu.VMEM((8, 256, 256), BF16),
            pltpu.VMEM((8, 256, 256), BF16),
            big,
            big,
            big,
            big,
            pltpu.VMEM((4, 8, 256, 256), BF16),
            pltpu.VMEM((256, 128), F32),
            pltpu.VMEM((4, 4, 128, 128), F32),
            pltpu.VMEM((4, 4, 128, 128), F32),
            pltpu.VMEM((256, 256), BF16),
            pltpu.VMEM((8, 128, 256), F32),
            pltpu.VMEM((slots, 32, 128), BF16),
            pltpu.VMEM((slots, 32, 128), BF16),
            pltpu.VMEM((6, 32, 128), F32),
            pltpu.VMEM((slots, 2, 128), F32),
            pltpu.VMEM((slots, 2, 128), F32),
            pltpu.VMEM((2, 2, 2, 128, 128), F32),
            pltpu.VMEM((nd, 2, 2, 64, 128), F32),
            dma((14,)),
            dma((2,)),
            dma((2,)),
            dma((2,)),
            dma((2,)),
            dma((nd,)),
            dma((nd,)),
            dma((2, 4)),
            dma((2, 4)),
            dma((2, 4)),
            dma((2, 4)),
            dma((nd,)),
            dma((nd,)),
        ],
        compiler_params=pltpu.CompilerParams(
            collective_id=0, has_side_effects=True, vmem_limit_bytes=62 * 1024 * 1024
        ),
        name="splat",
    )(
        features,
        jnp.transpose(geometry, (1, 0, 2)),
        picked,
        tile_ids,
        tile_lists,
        jnp.transpose(live_counts),
        cotangent,
    )

    feature_grads, geometry_grads, image_out = pl.pallas_call(
        owner_kernel,
        out_shape=(
            jax.ShapeDtypeStruct((blocks, 32, 128), F32),
            jax.ShapeDtypeStruct((6, 32, blocks), F32),
            jax.ShapeDtypeStruct((4, 64, 128), BF16),
        ),
        in_specs=[smem, vmem, vmem, vmem],
        out_specs=(vmem, vmem, vmem),
        scratch_shapes=[pltpu.VMEM((2, blocks, 128), F32)],
        name="owner",
    )(picked, grad_rx, ggeo_rx, image)
    return image_out, feature_grads, jnp.transpose(geometry_grads, (2, 0, 1))


def solution(mesh):
    placed = (
        P("tile", None, None),
        P("tile", None, None),
        P("tile", None, None),
        P("tile"),
        P("tile", "depth", None),
        P("tile", "depth"),
        P("tile", None, None),
    )
    return jax.shard_map(
        local,
        mesh=mesh,
        in_specs=placed,
        out_specs=(P("tile", "depth", None), P("tile", "depth", None), P("tile", None, "depth")),
        check_vma=False,
    )
```

```python
import functools

import jax
import jax.numpy as jnp
from jax import lax
from jax.experimental import pallas as pl
from jax.experimental.pallas import tpu as pltpu
from jax.sharding import PartitionSpec as P

MESH = pl.DeviceIdType.MESH
F32 = jnp.float32
BF16 = jnp.bfloat16
I32 = jnp.int32


def iota(shape, dim):
    return lax.broadcasted_iota(I32, shape, dim)


def ones_where(mask):
    return jnp.where(mask, 1.0, 0.0).astype(BF16)


def split_two(value):
    high = value.astype(BF16)
    low = (value - high.astype(F32)).astype(BF16)
    return high, low


def group_of(par, g, h):
    return (g // 2) * 8 + par * 4 + (g % 2) * 2 + h


def groups(step, many):
    def several(i, c):
        for k in range(many):
            step(i * many + k, c)
        return c

    lax.fori_loop(0, 8 // many, several, 0)


def chained(first, second, many):
    def several(i, c):
        coming = first(i * many)
        for k in range(many):
            ready = coming
            if k + 1 < many:
                coming = first(i * many + k + 1)
            second(i * many + k, ready)
        return c

    lax.fori_loop(0, 8 // many, several, 0)


def splat_kernel(
    nt,
    nd,
    cap,
    features,
    geometry,
    picked,
    tile_ids,
    tile_lists,
    live_counts,
    cotangent,
    image_out,
    grad_rx,
    ggeo_rx,
    own_feat,
    own_geo,
    feat_tx,
    feat_rx,
    feat_list,
    geo_rows,
    geo_tx,
    geo_rx,
    lists_rx,
    inv_vec,
    lists_sm,
    inv_sm,
    geo_part,
    geo,
    cot,
    cot_turned,
    place_mat,
    ahead_mat,
    behind_mat,
    fall,
    chain,
    thru,
    later,
    weights,
    sums,
    light,
    carry,
    offs,
    grad_sum,
    grad_list,
    grad_tx,
    moment,
    ggeo_list,
    ggeo_tx,
    image_part,
    image_rx,
    local_sem,
    geo_sem,
    feat_sem,
    grad_sem,
    ggeo_sem,
    lists_send,
    lists_recv,
    light_send,
    light_recv,
    carry_send,
    carry_recv,
    image_send,
    image_recv,
):
    me = lax.axis_index("tile")
    my = lax.axis_index("depth")
    slots = nt * cap
    near = my + 1 - 2 * (my % 2)
    far = nd - 1 - my

    def greet(i, c):
        pl.semaphore_signal(
            barrier, inc=1, device_id={"tile": lax.rem(me + i, nt)}, device_id_type=MESH
        )
        return c

    barrier = pltpu.get_barrier_semaphore()
    lax.fori_loop(1, nt, greet, 0)
    for step in range(1, nd):
        pl.semaphore_signal(
            barrier, inc=1, device_id={"depth": lax.rem(my + step, nd)}, device_id_type=MESH
        )

    fetch_geo = pltpu.make_async_copy(geometry, own_geo, local_sem.at[0])
    fetch_geo.start()
    fetch_feat = pltpu.make_async_copy(
        features.at[:, pl.ds(pl.multiple_of(my * 32, 32), 32), :], own_feat, local_sem.at[1]
    )
    fetch_feat.start()
    fetch_cot = []
    for par in range(2):
        for ph in range(2):
            for high in range(2):
                copy = pltpu.make_async_copy(
                    cotangent.at[high * 2 + par, pl.ds(ph * 128, 128), :],
                    cot.at[par * 2 + ph, pl.ds(high * 128, 128), :],
                    local_sem.at[5 + par * 4 + ph * 2 + high],
                )
                copy.start()
                fetch_cot.append(copy)

    lane8 = iota((8, 128), 1)
    listed = jnp.zeros((8, 128), I32)
    for u in range(4):
        for g in range(2):
            for k in range(8):
                listed = jnp.where(lane8 == u * 16 + g * 8 + k, tile_lists[u, g, k], listed)
            listed = jnp.where(lane8 == 64 + u * 2 + g, live_counts[g, u], listed)
    lists_rx[my] = listed

    fetch_geo.wait()
    lane_group = iota((slots, 128), 1) // 32
    for r in range(2):
        total = jnp.zeros((slots, 128), F32)
        for m in range(4 if r == 0 else 2):
            shift = lax.rem(32 * m + 128 - 32 * my, 128)
            total = jnp.where(lane_group == m, pltpu.roll(own_geo[4 * r + m], shift, 1), total)
        geo_rows[r] = total

    def pick_geo(t, c):
        for j in range(cap):
            at = picked[j, t]
            first = geo_rows[0, pl.ds(at, 1), :]
            second = geo_rows[1, pl.ds(at, 1), :]
            geo_tx[t * cap + j] = jnp.concatenate([first, second], axis=0)
        return c

    lax.fori_loop(0, nt, pick_geo, 0, unroll=4)
    mine = pl.multiple_of(me * cap, cap)
    geo_rx[pl.ds(mine, cap)] = geo_tx[pl.ds(mine, cap)]

    def across_depth(source, target, send, recv, peer):
        return pltpu.make_async_remote_copy(
            src_ref=source,
            dst_ref=target,
            send_sem=send,
            recv_sem=recv,
            device_id={"depth": peer},
            device_id_type=MESH,
        )

    def scatter_tiles(source, target, sem):
        def send(i, c):
            peer = lax.rem(me + i, nt)
            there = pl.multiple_of(peer * cap, cap)
            pltpu.make_async_remote_copy(
                src_ref=source.at[pl.ds(there, cap)],
                dst_ref=target.at[pl.ds(mine, cap)],
                send_sem=sem.at[0],
                recv_sem=sem.at[1],
                device_id={"tile": peer},
                device_id_type=MESH,
            ).start()
            return c

        lax.fori_loop(1, nt, send, 0)

    def all_tiles(source, target, sem):
        many = (nt - 1) * cap
        return pltpu.make_async_remote_copy(
            src_ref=source.at[pl.ds(0, many)],
            dst_ref=target.at[pl.ds(0, many)],
            send_sem=sem.at[0],
            recv_sem=sem.at[1],
            device_id={"tile": lax.rem(me + 1, nt)},
            device_id_type=MESH,
        )

    fetch_feat.wait()

    def pick_feat(t, c):
        for j in range(cap):
            feat_tx[t * cap + j] = own_feat[picked[j, t]]
        return c

    lax.fori_loop(0, nt, pick_feat, 0, unroll=4)
    feat_rx[pl.ds(mine, cap)] = feat_tx[pl.ds(mine, cap)]

    row_in = iota((256, 128), 0) % 128
    lane_out = iota((256, 128), 1)
    same_block = row_in // 32 == lane_out // 32
    before_mat = ones_where(same_block & (row_in < lane_out))
    after_mat = ones_where(same_block & (row_in > lane_out))
    place_key = lane_out - row_in // 32
    in_entry = iota((64, 256), 0)
    out_entry = iota((64, 256), 1) // 32

    def build(g, c):
        for h in range(2):
            place_mat[g * 2 + h] = ones_where(place_key == g * 8 + h * 4)
        want = out_entry + g * 8
        equal = ones_where(in_entry == want)
        less = ones_where(in_entry < want)
        more = ones_where(in_entry > want)
        ahead_mat[g] = jnp.concatenate([less, equal, less, equal], axis=0)
        behind_mat[g] = jnp.concatenate([more, equal, more, equal], axis=0)
        return c

    lax.fori_loop(0, 8, build, 0)

    for copy in fetch_cot:
        copy.wait()
    for chunk in range(4):
        cot_turned[chunk] = jnp.transpose(cot[chunk].astype(F32)).astype(BF16)

    pl.semaphore_wait(barrier, nt - 1 + nd - 1)
    for step in range(1, nd):
        peer = lax.rem(my + step, nd)
        across_depth(
            lists_rx.at[my], lists_rx.at[my], lists_send.at[peer], lists_recv.at[my], peer
        ).start()
    scatter_tiles(geo_tx, geo_rx, geo_sem)
    scatter_tiles(feat_tx, feat_rx, feat_sem)

    for step in range(1, nd):
        other = lax.rem(my + step, nd)
        across_depth(
            lists_rx.at[other], lists_rx.at[other], lists_send.at[other], lists_recv.at[other], other
        ).wait_recv()
    to_scalar = pltpu.make_async_copy(lists_rx, lists_sm, local_sem.at[2])
    to_scalar.start()
    slot_of_row = iota((128, 128), 0)
    lane = iota((128, 128), 1)
    found = jnp.zeros((128, 128), I32)
    for q in range(nd):
        row = jnp.broadcast_to(lists_rx[q, 0:1, :], (128, 128))
        hit = (row == slot_of_row) & (lane < 32)
        found = found + jnp.where(hit, lane + 32 * q, 0)
    for shift in (64, 32, 16, 8, 4, 2, 1):
        found = found + pltpu.roll(found, shift, 1)
    inv_vec[...] = jnp.transpose(found)[0:8]
    to_scalar.wait()
    inv_copy = pltpu.make_async_copy(inv_vec, inv_sm, local_sem.at[3])
    inv_copy.start()

    def within(index):
        return jnp.clip(index, 0, slots - 1)

    def slot_at(par, g, k):
        return within(lists_sm[g // 2, 0, par * 16 + (g % 2) * 8 + k])

    def live_at(tile, g):
        return lists_sm[g // 2, 0, 64 + tile * 2 + g % 2]

    all_tiles(geo_tx, geo_rx, geo_sem).wait_recv()

    def sort_geo(at, c):
        for k in range(8):
            rows = geo_rx[slot_at(at // 8, at % 8, k)]
            group = group_of(at // 8, at % 8, k // 4)
            for r in range(2):
                geo_part[r, k % 4, pl.ds(group, 1), :] = rows[r : r + 1, :]
        return c

    lax.fori_loop(0, 16, sort_geo, 0)
    lane_part = iota((32, 128), 1) // 32
    for p in range(6):
        r, m = p // 4, p % 4
        total = jnp.zeros((32, 128), F32)
        for i in range(4):
            shift = (32 * (i - m)) % 128
            part = geo_part[r, i]
            moved = pltpu.roll(part, shift, 1) if shift else part
            total = jnp.where(lane_part == i, moved, total)
        geo[p] = total

    column = iota((16, 128), 0).astype(F32) + 0.5
    entry_lane = iota((16, 128), 1) // 32
    left = iota((128, 128), 1) < 64

    def row_of(p, group):
        return jnp.broadcast_to(geo[p, pl.ds(group, 1), :], (16, 128))

    def origin(tile):
        return 16.0 * tile_ids[tile].astype(F32)

    def start_near(buffer, send, recv, chunk):
        whole = sums[...]
        buffer[chunk, 0] = jnp.where(left, whole[:128], pltpu.roll(whole[128:], 64, 1))
        across_depth(
            buffer.at[chunk, 0], buffer.at[chunk, 1], send.at[0, chunk], recv.at[0, chunk], near
        ).start()

    def start_far(buffer, send, recv, chunk):
        across_depth(
            buffer.at[chunk, 1], buffer.at[chunk, 1], send.at[0, chunk], recv.at[0, chunk], near
        ).wait_recv()
        buffer[chunk, 3] = buffer[chunk, 0] + buffer[chunk, 1]
        across_depth(
            buffer.at[chunk, 3], buffer.at[chunk, 2], send.at[1, chunk], recv.at[1, chunk], far
        ).start()

    def offsets_from(buffer, send, recv, chunk, use_near, use_far):
        across_depth(
            buffer.at[chunk, 2], buffer.at[chunk, 2], send.at[1, chunk], recv.at[1, chunk], far
        ).wait_recv()
        total = buffer[chunk, 3] + buffer[chunk, 2]
        same = use_near * buffer[chunk, 1] + use_far * buffer[chunk, 2]
        for high in range(2):
            if high == 0:
                both = jnp.where(left, total, pltpu.roll(same, 64, 1))
            else:
                both = jnp.where(left, pltpu.roll(total, 64, 1), same)
            top, rest = split_two(both)
            offs[pl.ds(high * 128, 128), :] = jnp.concatenate([top, rest], axis=1)

    odd = jnp.where(my % 2 == 1, 1.0, 0.0)
    upper = jnp.where(my >= 2, 1.0, 0.0)

    for chunk in range(4):
        par, ph = chunk // 2, chunk % 2
        sums[...] = jnp.zeros((256, 128), F32)

        def alpha_step(g, c, par=par, ph=ph, chunk=chunk):
            for h in range(2):
                group = group_of(par, g, h)
                mean_x, mean_y = row_of(0, group), row_of(1, group)
                half_a = -0.5 * row_of(2, group)
                minus_b = -row_of(3, group)
                half_c = -0.5 * row_of(4, group)
                opacity = row_of(5, group)
                highs, lows = [], []
                for high in range(2):
                    tile = high * 2 + par
                    dx = column - (mean_x - origin(tile))
                    alive = entry_lane + h * 4 < live_at(tile, g)
                    ax = jnp.where(alive, half_a * dx * dx, -1e30)
                    for py in range(8):
                        dy = (py + ph * 8 + 0.5) - mean_y
                        power = dx * (minus_b * dy) + (ax + half_c * dy * dy)
                        falloff = jnp.exp(power)
                        fall[chunk, g * 2 + h, pl.ds(high * 128 + py * 16, 16), :] = falloff
                        top, rest = split_two(jnp.log(1.0 - opacity * falloff))
                        highs.append(top)
                        lows.append(rest)
                both = jnp.concatenate(
                    [jnp.concatenate(highs, axis=0), jnp.concatenate(lows, axis=0)], axis=1
                )
                right = jnp.concatenate([before_mat, place_mat[g * 2 + h]], axis=1)
                result = jnp.dot(both, right, preferred_element_type=F32)
                chain[chunk, g * 2 + h] = result[:, :128]
                sums[...] += result[:, 128:]
            return c

        groups(alpha_step, 4)
        start_near(light, light_send, light_recv, chunk)
        if chunk >= 2:
            start_far(light, light_send, light_recv, chunk - 2)

    inv_copy.wait()

    for chunk in range(4):
        par, ph = chunk // 2, chunk % 2
        if 1 <= chunk <= 2:
            start_far(light, light_send, light_recv, chunk + 1)
        offsets_from(light, light_send, light_recv, chunk, odd, upper)

        def weight_ahead(g):
            return jnp.dot(offs[...], ahead_mat[g], preferred_element_type=F32)

        def weight_step(g, ahead, par=par, ph=ph, chunk=chunk):
            halves = []
            for h in range(2):
                group = group_of(par, g, h)
                opacity = jnp.broadcast_to(geo[5, pl.ds(group, 1), :], (256, 128))
                through = jnp.exp(chain[chunk, g * 2 + h] + ahead[:, h * 128 : (h + 1) * 128])
                thru[chunk, g * 2 + h] = through
                halves.append((through * (opacity * fall[chunk, g * 2 + h])).astype(BF16))
            weight = jnp.concatenate(halves, axis=1)
            weights[chunk, g] = weight
            grad = jnp.dot(cot_turned[chunk], weight, preferred_element_type=F32)
            if ph == 0:
                grad_sum[g] = grad
            else:
                grad = grad + grad_sum[g]
                at = (g // 2) * 4 + par * 2 + g % 2
                grad_list[pl.ds(pl.multiple_of(at * 8, 8), 8)] = jnp.transpose(grad).astype(
                    BF16
                ).reshape(8, 32, 128)

        chained(weight_ahead, weight_step, 4)

    def back_feat(k, c):
        grad_tx[k] = grad_list[within(inv_sm[0, k])]
        return c

    lax.fori_loop(0, slots, back_feat, 0, unroll=8)
    keep_own = pltpu.make_async_copy(
        grad_tx.at[pl.ds(mine, cap)], grad_rx.at[pl.ds(mine, cap)], local_sem.at[4]
    )
    keep_own.start()
    scatter_tiles(grad_tx, grad_rx, grad_sem)
    all_tiles(feat_tx, feat_rx, feat_sem).wait_recv()

    def sort_feat(at, c):
        for k in range(8):
            feat_list[at, pl.ds(k * 32, 32), :] = feat_rx[slot_at(at // 8, at % 8, k)]
        return c

    lax.fori_loop(0, 16, sort_feat, 0)
    image_part[...] = jnp.zeros(image_part.shape, F32)

    for chunk in range(4):
        par, ph = chunk // 2, chunk % 2
        sums[...] = jnp.zeros((256, 128), F32)

        def carry_ahead(g, par=par, ph=ph, chunk=chunk):
            feat = feat_list[par * 8 + g]
            shown = jnp.dot(weights[chunk, g], feat, preferred_element_type=F32)
            image_part[par, ph] += shown.reshape(2, 128, 128)
            return lax.dot_general(
                cot[chunk], feat, (((1,), (1,)), ((), ())), preferred_element_type=F32
            )

        def carry_step(g, dots, par=par, chunk=chunk):
            for h in range(2):
                group = group_of(par, g, h)
                opacity = jnp.broadcast_to(geo[5, pl.ds(group, 1), :], (256, 128))
                direct = dots[:, h * 128 : (h + 1) * 128] * thru[chunk, g * 2 + h]
                chain[chunk, g * 2 + h] = direct
                top, rest = split_two(direct * (opacity * fall[chunk, g * 2 + h]))
                both = jnp.concatenate([top, rest], axis=1)
                right = jnp.concatenate([after_mat, place_mat[g * 2 + h]], axis=1)
                result = jnp.dot(both, right, preferred_element_type=F32)
                later[chunk, g * 2 + h] = result[:, :128]
                sums[...] += result[:, 128:]

        chained(carry_ahead, carry_step, 4)
        start_near(carry, carry_send, carry_recv, chunk)
        if chunk:
            start_far(carry, carry_send, carry_recv, chunk - 1)

    for chunk in range(4):
        par, ph = chunk // 2, chunk % 2
        if chunk == 1:
            start_far(carry, carry_send, carry_recv, 3)
            for step in range(1, nd):
                peer = lax.rem(my + step, nd)
                across_depth(
                    image_part.at[
                        :, peer // 2, :, pl.ds(pl.multiple_of((peer % 2) * 64, 64), 64), :
                    ],
                    image_rx.at[my],
                    image_send.at[peer],
                    image_recv.at[my],
                    peer,
                ).start()
        offsets_from(carry, carry_send, carry_recv, chunk, 1.0 - odd, 1.0 - upper)

        def shape_step(g, c, par=par, ph=ph, chunk=chunk):
            behind = jnp.dot(offs[...], behind_mat[g], preferred_element_type=F32)
            for h in range(2):
                group = group_of(par, g, h)
                mean_x, mean_y = row_of(0, group), row_of(1, group)
                opacity = row_of(5, group)
                parts = [jnp.zeros((16, 128), F32) for _ in range(6)]
                for high in range(2):
                    tile = high * 2 + par
                    dx = column - (mean_x - origin(tile))
                    flat = jnp.zeros((16, 128), F32)
                    tilt = jnp.zeros((16, 128), F32)
                    bend = jnp.zeros((16, 128), F32)
                    for py in range(8):
                        at = high * 128 + py * 16
                        rows = pl.ds(at, 16)
                        dy = (py + ph * 8 + 0.5) - mean_y
                        falloff = fall[chunk, g * 2 + h, rows, :]
                        after = (
                            later[chunk, g * 2 + h, rows, :]
                            + behind[at : at + 16, h * 128 : (h + 1) * 128]
                        )
                        alpha_grad = chain[chunk, g * 2 + h, rows, :] - after / (
                            1.0 - opacity * falloff
                        )
                        term = alpha_grad * falloff
                        term_y = term * dy
                        flat = flat + term
                        tilt = tilt + term_y
                        bend = bend + term_y * dy
                    flat_x = flat * dx
                    adds = [flat, flat_x, tilt, flat_x * dx, tilt * dx, bend]
                    parts = [a + b for a, b in zip(parts, adds)]
                for i, part in enumerate(parts):
                    folded = jnp.sum(part, axis=0, keepdims=True)
                    if ph:
                        folded = folded + moment[i, pl.ds(group, 1), :]
                    moment[i, pl.ds(group, 1), :] = folded
            return c

        groups(shape_step, 4)

    one, sx, sy, sxx, sxy, syy = [moment[i] for i in range(6)]
    conic_a, conic_b, conic_c, opac = [geo[p] for p in (2, 3, 4, 5)]
    ggeo = [
        opac * (conic_a * sx + conic_b * sy),
        opac * (conic_b * sx + conic_c * sy),
        -0.5 * opac * sxx,
        -opac * sxy,
        -0.5 * opac * syy,
        one,
    ]
    for i in range(4):
        for r in range(2):
            total = jnp.zeros((32, 128), F32)
            for m in range(4 if r == 0 else 2):
                shift = (32 * (m - i)) % 128
                part = ggeo[4 * r + m]
                moved = pltpu.roll(part, shift, 1) if shift else part
                total = jnp.where(lane_part == m, moved, total)
            for group in range(32):
                ggeo_list[group * 4 + i, r : r + 1, :] = total[group : group + 1]

    def back_geo(k, c):
        ggeo_tx[k] = ggeo_list[within(inv_sm[0, k])]
        return c

    lax.fori_loop(0, slots, back_geo, 0, unroll=8)
    keep_geo = pltpu.make_async_copy(
        ggeo_tx.at[pl.ds(mine, cap)], ggeo_rx.at[pl.ds(mine, cap)], local_sem.at[13]
    )
    keep_geo.start()
    scatter_tiles(ggeo_tx, ggeo_rx, ggeo_sem)

    image = image_part[:, my // 2, :, pl.ds(pl.multiple_of((my % 2) * 64, 64), 64), :]
    for step in range(1, nd):
        other = lax.rem(my + step, nd)
        across_depth(
            image_rx.at[other], image_rx.at[other], image_send.at[other], image_recv.at[other], other
        ).wait_recv()
        image = image + image_rx[other]
    for par in range(2):
        for high in range(2):
            image_out[high * 2 + par] = image[par, high].astype(BF16)

    for step in range(1, nd):
        other = lax.rem(my + step, nd)
        across_depth(
            lists_rx.at[other], lists_rx.at[other], lists_send.at[other], lists_recv.at[other], other
        ).wait_send()
        across_depth(
            image_rx.at[other], image_rx.at[other], image_send.at[other], image_recv.at[other], other
        ).wait_send()
    for buffer, send, recv in ((light, light_send, light_recv), (carry, carry_send, carry_recv)):
        for chunk in range(4):
            across_depth(
                buffer.at[chunk, 0], buffer.at[chunk, 1], send.at[0, chunk], recv.at[0, chunk], near
            ).wait_send()
            across_depth(
                buffer.at[chunk, 3], buffer.at[chunk, 2], send.at[1, chunk], recv.at[1, chunk], far
            ).wait_send()
    all_tiles(geo_tx, geo_rx, geo_sem).wait_send()
    all_tiles(feat_tx, feat_rx, feat_sem).wait_send()
    keep_own.wait()
    keep_geo.wait()
    all_tiles(grad_tx, grad_rx, grad_sem).wait()
    all_tiles(ggeo_tx, ggeo_rx, ggeo_sem).wait()


def owner_kernel(picked, grad_rx, ggeo_rx, image, grad_out, ggeo_out, image_out, rows):
    cap, nt = picked.shape
    image_out[...] = image[...]

    def put(t, c):
        for j in range(cap):
            k = t * cap + j
            at = picked[j, t]
            grad_out[at] = grad_rx[k].astype(F32)
            for r in range(2):
                rows[r, pl.ds(at, 1), :] = ggeo_rx[k, r : r + 1, :]
        return c

    lax.fori_loop(0, nt, put, 0, unroll=4)
    for r in range(2):
        turned = jnp.transpose(rows[r])
        for m in range(4 if r == 0 else 2):
            ggeo_out[4 * r + m] = turned[m * 32 : m * 32 + 32]


def local(features, geometry, send_lists, tile_ids, tile_lists, live_counts, cotangent):
    nt, nd = lax.axis_size("tile"), lax.axis_size("depth")
    cap = send_lists.shape[2]
    slots = nt * cap
    blocks = features.shape[0]
    picked = jnp.transpose(send_lists[0])

    vmem = pl.BlockSpec(memory_space=pltpu.VMEM)
    smem = pl.BlockSpec(memory_space=pltpu.SMEM)
    hbm = pl.BlockSpec(memory_space=pl.ANY)
    dma = pltpu.SemaphoreType.DMA
    big = pltpu.VMEM((4, 16, 256, 128), F32)
    image, grad_rx, ggeo_rx = pl.pallas_call(
        functools.partial(splat_kernel, nt, nd, cap),
        out_shape=(
            jax.ShapeDtypeStruct((4, 64, 128), BF16),
            jax.ShapeDtypeStruct((slots, 32, 128), BF16),
            jax.ShapeDtypeStruct((slots, 2, 128), F32),
        ),
        in_specs=[hbm, hbm, smem, smem, smem, smem, hbm],
        out_specs=(vmem, hbm, hbm),
        scratch_shapes=[
            pltpu.VMEM((blocks, 32, 128), BF16),
            pltpu.VMEM((6, blocks, 128), F32),
            pltpu.VMEM((slots, 32, 128), BF16),
            pltpu.VMEM((slots, 32, 128), BF16),
            pltpu.VMEM((16, 256, 128), BF16),
            pltpu.VMEM((2, blocks, 128), F32),
            pltpu.VMEM((slots, 2, 128), F32),
            pltpu.VMEM((slots, 2, 128), F32),
            pltpu.VMEM((nd, 8, 128), I32),
            pltpu.VMEM((8, 128), I32),
            pltpu.SMEM((nd, 8, 128), I32),
            pltpu.SMEM((8, 128), I32),
            pltpu.VMEM((2, 4, 32, 128), F32),
            pltpu.VMEM((6, 32, 128), F32),
            pltpu.VMEM((4, 256, 128), BF16),
            pltpu.VMEM((4, 128, 256), BF16),
            pltpu.VMEM((16, 256, 128), BF16),
            pltpu.VMEM((8, 256, 256), BF16),
            pltpu.VMEM((8, 256, 256), BF16),
            big,
            big,
            big,
            big,
            pltpu.VMEM((4, 8, 256, 256), BF16),
            pltpu.VMEM((256, 128), F32),
            pltpu.VMEM((4, 4, 128, 128), F32),
            pltpu.VMEM((4, 4, 128, 128), F32),
            pltpu.VMEM((256, 256), BF16),
            pltpu.VMEM((8, 128, 256), F32),
            pltpu.VMEM((slots, 32, 128), BF16),
            pltpu.VMEM((slots, 32, 128), BF16),
            pltpu.VMEM((6, 32, 128), F32),
            pltpu.VMEM((slots, 2, 128), F32),
            pltpu.VMEM((slots, 2, 128), F32),
            pltpu.VMEM((2, 2, 2, 128, 128), F32),
            pltpu.VMEM((nd, 2, 2, 64, 128), F32),
            dma((14,)),
            dma((2,)),
            dma((2,)),
            dma((2,)),
            dma((2,)),
            dma((nd,)),
            dma((nd,)),
            dma((2, 4)),
            dma((2, 4)),
            dma((2, 4)),
            dma((2, 4)),
            dma((nd,)),
            dma((nd,)),
        ],
        compiler_params=pltpu.CompilerParams(
            collective_id=0, has_side_effects=True, vmem_limit_bytes=62 * 1024 * 1024
        ),
        name="splat",
    )(
        features,
        jnp.transpose(geometry, (1, 0, 2)),
        picked,
        tile_ids,
        tile_lists,
        jnp.transpose(live_counts),
        cotangent,
    )

    feature_grads, geometry_grads, image_out = pl.pallas_call(
        owner_kernel,
        out_shape=(
            jax.ShapeDtypeStruct((blocks, 32, 128), F32),
            jax.ShapeDtypeStruct((6, 32, blocks), F32),
            jax.ShapeDtypeStruct((4, 64, 128), BF16),
        ),
        in_specs=[smem, vmem, vmem, vmem],
        out_specs=(vmem, vmem, vmem),
        scratch_shapes=[pltpu.VMEM((2, blocks, 128), F32)],
        name="owner",
    )(picked, grad_rx, ggeo_rx, image)
    return image_out, feature_grads, jnp.transpose(geometry_grads, (2, 0, 1))


def solution(mesh):
    placed = (
        P("tile", None, None),
        P("tile", None, None),
        P("tile", None, None),
        P("tile"),
        P("tile", "depth", None),
        P("tile", "depth"),
        P("tile", None, None),
    )
    return jax.shard_map(
        local,
        mesh=mesh,
        in_specs=placed,
        out_specs=(P("tile", "depth", None), P("tile", "depth", None), P("tile", None, "depth")),
        check_vma=False,
    )
```

```python
import functools

import jax
import jax.numpy as jnp
from jax import lax
from jax.experimental import pallas as pl
from jax.experimental.pallas import tpu as pltpu
from jax.sharding import PartitionSpec as P

MESH = pl.DeviceIdType.MESH
F32 = jnp.float32
BF16 = jnp.bfloat16
I32 = jnp.int32


def iota(shape, dim):
    return lax.broadcasted_iota(I32, shape, dim)


def ones_where(mask):
    return jnp.where(mask, 1.0, 0.0).astype(BF16)


def split_two(value):
    high = value.astype(BF16)
    low = (value - high.astype(F32)).astype(BF16)
    return high, low


def group_of(par, g, h):
    return (g // 2) * 8 + par * 4 + (g % 2) * 2 + h


def groups(step, many):
    def several(i, c):
        for k in range(many):
            step(i * many + k, c)
        return c

    lax.fori_loop(0, 8 // many, several, 0)


def chained(first, second, many):
    def several(i, c):
        coming = first(i * many)
        for k in range(many):
            ready = coming
            if k + 1 < many:
                coming = first(i * many + k + 1)
            second(i * many + k, ready)
        return c

    lax.fori_loop(0, 8 // many, several, 0)


def splat_kernel(
    nt,
    nd,
    cap,
    features,
    geometry,
    picked,
    tile_ids,
    tile_lists,
    live_counts,
    cotangent,
    image_out,
    grad_rx,
    ggeo_rx,
    own_feat,
    own_geo,
    feat_tx,
    feat_rx,
    feat_list,
    geo_rows,
    geo_tx,
    geo_rx,
    lists_rx,
    inv_vec,
    lists_sm,
    inv_sm,
    geo_part,
    geo,
    cot,
    cot_turned,
    place_mat,
    ahead_mat,
    behind_mat,
    fall,
    chain,
    thru,
    later,
    weights,
    sums,
    light,
    carry,
    offs,
    grad_sum,
    grad_list,
    grad_tx,
    moment,
    ggeo_list,
    ggeo_tx,
    image_part,
    image_rx,
    local_sem,
    geo_sem,
    feat_sem,
    grad_sem,
    ggeo_sem,
    lists_send,
    lists_recv,
    light_send,
    light_recv,
    carry_send,
    carry_recv,
    image_send,
    image_recv,
):
    me = lax.axis_index("tile")
    my = lax.axis_index("depth")
    slots = nt * cap
    near = my + 1 - 2 * (my % 2)
    far = nd - 1 - my

    def greet(i, c):
        pl.semaphore_signal(
            barrier, inc=1, device_id={"tile": lax.rem(me + i, nt)}, device_id_type=MESH
        )
        return c

    barrier = pltpu.get_barrier_semaphore()
    lax.fori_loop(1, nt, greet, 0)
    for step in range(1, nd):
        pl.semaphore_signal(
            barrier, inc=1, device_id={"depth": lax.rem(my + step, nd)}, device_id_type=MESH
        )

    fetch_geo = pltpu.make_async_copy(geometry, own_geo, local_sem.at[0])
    fetch_geo.start()
    fetch_feat = pltpu.make_async_copy(
        features.at[:, pl.ds(pl.multiple_of(my * 32, 32), 32), :], own_feat, local_sem.at[1]
    )
    fetch_feat.start()
    fetch_cot = []
    for par in range(2):
        for ph in range(2):
            for high in range(2):
                copy = pltpu.make_async_copy(
                    cotangent.at[high * 2 + par, pl.ds(ph * 128, 128), :],
                    cot.at[par * 2 + ph, pl.ds(high * 128, 128), :],
                    local_sem.at[5 + par * 4 + ph * 2 + high],
                )
                copy.start()
                fetch_cot.append(copy)

    lane8 = iota((8, 128), 1)
    listed = jnp.zeros((8, 128), I32)
    for u in range(4):
        for g in range(2):
            for k in range(8):
                listed = jnp.where(lane8 == u * 16 + g * 8 + k, tile_lists[u, g, k], listed)
            listed = jnp.where(lane8 == 64 + u * 2 + g, live_counts[g, u], listed)
    lists_rx[my] = listed

    fetch_geo.wait()
    lane_group = iota((slots, 128), 1) // 32
    for r in range(2):
        total = jnp.zeros((slots, 128), F32)
        for m in range(4 if r == 0 else 2):
            shift = lax.rem(32 * m + 128 - 32 * my, 128)
            total = jnp.where(lane_group == m, pltpu.roll(own_geo[4 * r + m], shift, 1), total)
        geo_rows[r] = total

    def pick_geo(t, c):
        for j in range(cap):
            at = picked[j, t]
            first = geo_rows[0, pl.ds(at, 1), :]
            second = geo_rows[1, pl.ds(at, 1), :]
            geo_tx[t * cap + j] = jnp.concatenate([first, second], axis=0)
        return c

    lax.fori_loop(0, nt, pick_geo, 0, unroll=4)
    mine = pl.multiple_of(me * cap, cap)
    geo_rx[pl.ds(mine, cap)] = geo_tx[pl.ds(mine, cap)]

    def across_depth(source, target, send, recv, peer):
        return pltpu.make_async_remote_copy(
            src_ref=source,
            dst_ref=target,
            send_sem=send,
            recv_sem=recv,
            device_id={"depth": peer},
            device_id_type=MESH,
        )

    def scatter_tiles(source, target, sem):
        def send(i, c):
            peer = lax.rem(me + i, nt)
            there = pl.multiple_of(peer * cap, cap)
            pltpu.make_async_remote_copy(
                src_ref=source.at[pl.ds(there, cap)],
                dst_ref=target.at[pl.ds(mine, cap)],
                send_sem=sem.at[0],
                recv_sem=sem.at[1],
                device_id={"tile": peer},
                device_id_type=MESH,
            ).start()
            return c

        lax.fori_loop(1, nt, send, 0)

    def all_tiles(source, target, sem):
        many = (nt - 1) * cap
        return pltpu.make_async_remote_copy(
            src_ref=source.at[pl.ds(0, many)],
            dst_ref=target.at[pl.ds(0, many)],
            send_sem=sem.at[0],
            recv_sem=sem.at[1],
            device_id={"tile": lax.rem(me + 1, nt)},
            device_id_type=MESH,
        )

    fetch_feat.wait()

    def pick_feat(t, c):
        for j in range(cap):
            feat_tx[t * cap + j] = own_feat[picked[j, t]]
        return c

    lax.fori_loop(0, nt, pick_feat, 0, unroll=4)
    feat_rx[pl.ds(mine, cap)] = feat_tx[pl.ds(mine, cap)]

    row_in = iota((256, 128), 0) % 128
    lane_out = iota((256, 128), 1)
    same_block = row_in // 32 == lane_out // 32
    before_mat = ones_where(same_block & (row_in < lane_out))
    after_mat = ones_where(same_block & (row_in > lane_out))
    place_key = lane_out - row_in // 32
    in_entry = iota((64, 256), 0)
    out_entry = iota((64, 256), 1) // 32

    def build(g, c):
        for h in range(2):
            place_mat[g * 2 + h] = ones_where(place_key == g * 8 + h * 4)
        want = out_entry + g * 8
        equal = ones_where(in_entry == want)
        less = ones_where(in_entry < want)
        more = ones_where(in_entry > want)
        ahead_mat[g] = jnp.concatenate([less, equal, less, equal], axis=0)
        behind_mat[g] = jnp.concatenate([more, equal, more, equal], axis=0)
        return c

    lax.fori_loop(0, 8, build, 0)

    for copy in fetch_cot:
        copy.wait()
    for chunk in range(4):
        cot_turned[chunk] = jnp.transpose(cot[chunk].astype(F32)).astype(BF16)

    pl.semaphore_wait(barrier, nt - 1 + nd - 1)
    for step in range(1, nd):
        peer = lax.rem(my + step, nd)
        across_depth(
            lists_rx.at[my], lists_rx.at[my], lists_send.at[peer], lists_recv.at[my], peer
        ).start()
    scatter_tiles(geo_tx, geo_rx, geo_sem)
    scatter_tiles(feat_tx, feat_rx, feat_sem)

    for step in range(1, nd):
        other = lax.rem(my + step, nd)
        across_depth(
            lists_rx.at[other], lists_rx.at[other], lists_send.at[other], lists_recv.at[other], other
        ).wait_recv()
    to_scalar = pltpu.make_async_copy(lists_rx, lists_sm, local_sem.at[2])
    to_scalar.start()
    slot_of_row = iota((128, 128), 0)
    lane = iota((128, 128), 1)
    found = jnp.zeros((128, 128), I32)
    for q in range(nd):
        row = jnp.broadcast_to(lists_rx[q, 0:1, :], (128, 128))
        hit = (row == slot_of_row) & (lane < 32)
        found = found + jnp.where(hit, lane + 32 * q, 0)
    for shift in (64, 32, 16, 8, 4, 2, 1):
        found = found + pltpu.roll(found, shift, 1)
    inv_vec[...] = jnp.transpose(found)[0:8]
    to_scalar.wait()
    inv_copy = pltpu.make_async_copy(inv_vec, inv_sm, local_sem.at[3])
    inv_copy.start()

    def within(index):
        return jnp.clip(index, 0, slots - 1)

    def slot_at(par, g, k):
        return within(lists_sm[g // 2, 0, par * 16 + (g % 2) * 8 + k])

    def live_at(tile, g):
        return lists_sm[g // 2, 0, 64 + tile * 2 + g % 2]

    all_tiles(geo_tx, geo_rx, geo_sem).wait_recv()

    def sort_geo(at, c):
        for k in range(8):
            rows = geo_rx[slot_at(at // 8, at % 8, k)]
            group = group_of(at // 8, at % 8, k // 4)
            for r in range(2):
                geo_part[r, k % 4, pl.ds(group, 1), :] = rows[r : r + 1, :]
        return c

    lax.fori_loop(0, 16, sort_geo, 0)
    lane_part = iota((32, 128), 1) // 32
    for p in range(6):
        r, m = p // 4, p % 4
        total = jnp.zeros((32, 128), F32)
        for i in range(4):
            shift = (32 * (i - m)) % 128
            part = geo_part[r, i]
            moved = pltpu.roll(part, shift, 1) if shift else part
            total = jnp.where(lane_part == i, moved, total)
        geo[p] = total

    column = iota((16, 128), 0).astype(F32) + 0.5
    entry_lane = iota((16, 128), 1) // 32
    left = iota((128, 128), 1) < 64

    def row_of(p, group):
        return jnp.broadcast_to(geo[p, pl.ds(group, 1), :], (16, 128))

    def origin(tile):
        return 16.0 * tile_ids[tile].astype(F32)

    def start_near(buffer, send, recv, chunk):
        whole = sums[...]
        buffer[chunk, 0] = jnp.where(left, whole[:128], pltpu.roll(whole[128:], 64, 1))
        across_depth(
            buffer.at[chunk, 0], buffer.at[chunk, 1], send.at[0, chunk], recv.at[0, chunk], near
        ).start()

    def start_far(buffer, send, recv, chunk):
        across_depth(
            buffer.at[chunk, 1], buffer.at[chunk, 1], send.at[0, chunk], recv.at[0, chunk], near
        ).wait_recv()
        buffer[chunk, 3] = buffer[chunk, 0] + buffer[chunk, 1]
        across_depth(
            buffer.at[chunk, 3], buffer.at[chunk, 2], send.at[1, chunk], recv.at[1, chunk], far
        ).start()

    def offsets_from(buffer, send, recv, chunk, use_near, use_far):
        across_depth(
            buffer.at[chunk, 2], buffer.at[chunk, 2], send.at[1, chunk], recv.at[1, chunk], far
        ).wait_recv()
        total = buffer[chunk, 3] + buffer[chunk, 2]
        same = use_near * buffer[chunk, 1] + use_far * buffer[chunk, 2]
        for high in range(2):
            if high == 0:
                both = jnp.where(left, total, pltpu.roll(same, 64, 1))
            else:
                both = jnp.where(left, pltpu.roll(total, 64, 1), same)
            top, rest = split_two(both)
            offs[pl.ds(high * 128, 128), :] = jnp.concatenate([top, rest], axis=1)

    odd = jnp.where(my % 2 == 1, 1.0, 0.0)
    upper = jnp.where(my >= 2, 1.0, 0.0)

    def phase_1(par, c):
        for ph in range(2):
            chunk = par * 2 + ph
            sums[...] = jnp.zeros((256, 128), F32)

            def alpha_step(g, c, par=par, ph=ph, chunk=chunk):
                for h in range(2):
                    group = group_of(par, g, h)
                    mean_x, mean_y = row_of(0, group), row_of(1, group)
                    half_a = -0.5 * row_of(2, group)
                    minus_b = -row_of(3, group)
                    half_c = -0.5 * row_of(4, group)
                    opacity = row_of(5, group)
                    highs, lows = [], []
                    for high in range(2):
                        tile = high * 2 + par
                        dx = column - (mean_x - origin(tile))
                        alive = entry_lane + h * 4 < live_at(tile, g)
                        ax = jnp.where(alive, half_a * dx * dx, -1e30)
                        for py in range(8):
                            dy = (py + ph * 8 + 0.5) - mean_y
                            power = dx * (minus_b * dy) + (ax + half_c * dy * dy)
                            falloff = jnp.exp(power)
                            fall[chunk, g * 2 + h, pl.ds(high * 128 + py * 16, 16), :] = falloff
                            top, rest = split_two(jnp.log(1.0 - opacity * falloff))
                            highs.append(top)
                            lows.append(rest)
                    both = jnp.concatenate(
                        [jnp.concatenate(highs, axis=0), jnp.concatenate(lows, axis=0)], axis=1
                    )
                    right = jnp.concatenate([before_mat, place_mat[g * 2 + h]], axis=1)
                    result = jnp.dot(both, right, preferred_element_type=F32)
                    chain[chunk, g * 2 + h] = result[:, :128]
                    sums[...] += result[:, 128:]
                return c

            groups(alpha_step, 4)
            start_near(light, light_send, light_recv, chunk)

            @pl.when(par == 1)
            def _(ph=ph):
                start_far(light, light_send, light_recv, ph)
        return c

    lax.fori_loop(0, 2, phase_1, 0)

    inv_copy.wait()

    def phase_2(par, c):
        for ph in range(2):
            chunk = par * 2 + ph
            @pl.when(par == 1 - ph)
            def _(ph=ph):
                start_far(light, light_send, light_recv, 3 - ph)

            offsets_from(light, light_send, light_recv, chunk, odd, upper)

            def weight_ahead(g):
                return jnp.dot(offs[...], ahead_mat[g], preferred_element_type=F32)

            def weight_step(g, ahead, par=par, ph=ph, chunk=chunk):
                halves = []
                for h in range(2):
                    group = group_of(par, g, h)
                    opacity = jnp.broadcast_to(geo[5, pl.ds(group, 1), :], (256, 128))
                    through = jnp.exp(chain[chunk, g * 2 + h] + ahead[:, h * 128 : (h + 1) * 128])
                    thru[chunk, g * 2 + h] = through
                    halves.append((through * (opacity * fall[chunk, g * 2 + h])).astype(BF16))
                weight = jnp.concatenate(halves, axis=1)
                weights[chunk, g] = weight
                grad = jnp.dot(cot_turned[chunk], weight, preferred_element_type=F32)
                if ph == 0:
                    grad_sum[g] = grad
                else:
                    grad = grad + grad_sum[g]
                    at = (g // 2) * 4 + par * 2 + g % 2
                    grad_list[pl.ds(pl.multiple_of(at * 8, 8), 8)] = jnp.transpose(grad).astype(
                        BF16
                    ).reshape(8, 32, 128)

            chained(weight_ahead, weight_step, 4)
        return c

    lax.fori_loop(0, 2, phase_2, 0)

    def back_feat(k, c):
        grad_tx[k] = grad_list[within(inv_sm[0, k])]
        return c

    lax.fori_loop(0, slots, back_feat, 0, unroll=8)
    keep_own = pltpu.make_async_copy(
        grad_tx.at[pl.ds(mine, cap)], grad_rx.at[pl.ds(mine, cap)], local_sem.at[4]
    )
    keep_own.start()
    scatter_tiles(grad_tx, grad_rx, grad_sem)
    all_tiles(feat_tx, feat_rx, feat_sem).wait_recv()

    def sort_feat(at, c):
        for k in range(8):
            feat_list[at, pl.ds(k * 32, 32), :] = feat_rx[slot_at(at // 8, at % 8, k)]
        return c

    lax.fori_loop(0, 16, sort_feat, 0)
    image_part[...] = jnp.zeros(image_part.shape, F32)

    def phase_3(par, c):
        for ph in range(2):
            chunk = par * 2 + ph
            sums[...] = jnp.zeros((256, 128), F32)

            def carry_ahead(g, par=par, ph=ph, chunk=chunk):
                feat = feat_list[par * 8 + g]
                shown = jnp.dot(weights[chunk, g], feat, preferred_element_type=F32)
                image_part[par, ph] += shown.reshape(2, 128, 128)
                return lax.dot_general(
                    cot[chunk], feat, (((1,), (1,)), ((), ())), preferred_element_type=F32
                )

            def carry_step(g, dots, par=par, chunk=chunk):
                for h in range(2):
                    group = group_of(par, g, h)
                    opacity = jnp.broadcast_to(geo[5, pl.ds(group, 1), :], (256, 128))
                    direct = dots[:, h * 128 : (h + 1) * 128] * thru[chunk, g * 2 + h]
                    chain[chunk, g * 2 + h] = direct
                    top, rest = split_two(direct * (opacity * fall[chunk, g * 2 + h]))
                    both = jnp.concatenate([top, rest], axis=1)
                    right = jnp.concatenate([after_mat, place_mat[g * 2 + h]], axis=1)
                    result = jnp.dot(both, right, preferred_element_type=F32)
                    later[chunk, g * 2 + h] = result[:, :128]
                    sums[...] += result[:, 128:]

            chained(carry_ahead, carry_step, 4)
            start_near(carry, carry_send, carry_recv, chunk)
            if ph:
                start_far(carry, carry_send, carry_recv, par * 2)
            else:

                @pl.when(par == 1)
                def _():
                    start_far(carry, carry_send, carry_recv, 1)
        return c

    lax.fori_loop(0, 2, phase_3, 0)

    def phase_4(par, c):
        for ph in range(2):
            chunk = par * 2 + ph
            if ph:

                @pl.when(par == 0)
                def _():
                    start_far(carry, carry_send, carry_recv, 3)
                    for step in range(1, nd):
                        peer = lax.rem(my + step, nd)
                        across_depth(
                            image_part.at[
                                :, peer // 2, :, pl.ds(pl.multiple_of((peer % 2) * 64, 64), 64), :
                            ],
                            image_rx.at[my],
                            image_send.at[peer],
                            image_recv.at[my],
                            peer,
                        ).start()

            offsets_from(carry, carry_send, carry_recv, chunk, 1.0 - odd, 1.0 - upper)

            def shape_step(g, c, par=par, ph=ph, chunk=chunk):
                behind = jnp.dot(offs[...], behind_mat[g], preferred_element_type=F32)
                for h in range(2):
                    group = group_of(par, g, h)
                    mean_x, mean_y = row_of(0, group), row_of(1, group)
                    opacity = row_of(5, group)
                    parts = [jnp.zeros((16, 128), F32) for _ in range(6)]
                    for high in range(2):
                        tile = high * 2 + par
                        dx = column - (mean_x - origin(tile))
                        flat = jnp.zeros((16, 128), F32)
                        tilt = jnp.zeros((16, 128), F32)
                        bend = jnp.zeros((16, 128), F32)
                        for py in range(8):
                            at = high * 128 + py * 16
                            rows = pl.ds(at, 16)
                            dy = (py + ph * 8 + 0.5) - mean_y
                            falloff = fall[chunk, g * 2 + h, rows, :]
                            after = (
                                later[chunk, g * 2 + h, rows, :]
                                + behind[at : at + 16, h * 128 : (h + 1) * 128]
                            )
                            alpha_grad = chain[chunk, g * 2 + h, rows, :] - after / (
                                1.0 - opacity * falloff
                            )
                            term = alpha_grad * falloff
                            term_y = term * dy
                            flat = flat + term
                            tilt = tilt + term_y
                            bend = bend + term_y * dy
                        flat_x = flat * dx
                        adds = [flat, flat_x, tilt, flat_x * dx, tilt * dx, bend]
                        parts = [a + b for a, b in zip(parts, adds)]
                    for i, part in enumerate(parts):
                        folded = jnp.sum(part, axis=0, keepdims=True)
                        if ph:
                            folded = folded + moment[i, pl.ds(group, 1), :]
                        moment[i, pl.ds(group, 1), :] = folded
                return c

            groups(shape_step, 4)
        return c

    lax.fori_loop(0, 2, phase_4, 0)

    one, sx, sy, sxx, sxy, syy = [moment[i] for i in range(6)]
    conic_a, conic_b, conic_c, opac = [geo[p] for p in (2, 3, 4, 5)]
    ggeo = [
        opac * (conic_a * sx + conic_b * sy),
        opac * (conic_b * sx + conic_c * sy),
        -0.5 * opac * sxx,
        -opac * sxy,
        -0.5 * opac * syy,
        one,
    ]
    for i in range(4):
        for r in range(2):
            total = jnp.zeros((32, 128), F32)
            for m in range(4 if r == 0 else 2):
                shift = (32 * (m - i)) % 128
                part = ggeo[4 * r + m]
                moved = pltpu.roll(part, shift, 1) if shift else part
                total = jnp.where(lane_part == m, moved, total)
            for group in range(32):
                ggeo_list[group * 4 + i, r : r + 1, :] = total[group : group + 1]

    def back_geo(k, c):
        ggeo_tx[k] = ggeo_list[within(inv_sm[0, k])]
        return c

    lax.fori_loop(0, slots, back_geo, 0, unroll=8)
    keep_geo = pltpu.make_async_copy(
        ggeo_tx.at[pl.ds(mine, cap)], ggeo_rx.at[pl.ds(mine, cap)], local_sem.at[13]
    )
    keep_geo.start()
    scatter_tiles(ggeo_tx, ggeo_rx, ggeo_sem)

    image = image_part[:, my // 2, :, pl.ds(pl.multiple_of((my % 2) * 64, 64), 64), :]
    for step in range(1, nd):
        other = lax.rem(my + step, nd)
        across_depth(
            image_rx.at[other], image_rx.at[other], image_send.at[other], image_recv.at[other], other
        ).wait_recv()
        image = image + image_rx[other]
    for par in range(2):
        for high in range(2):
            image_out[high * 2 + par] = image[par, high].astype(BF16)

    for step in range(1, nd):
        other = lax.rem(my + step, nd)
        across_depth(
            lists_rx.at[other], lists_rx.at[other], lists_send.at[other], lists_recv.at[other], other
        ).wait_send()
        across_depth(
            image_rx.at[other], image_rx.at[other], image_send.at[other], image_recv.at[other], other
        ).wait_send()
    for buffer, send, recv in ((light, light_send, light_recv), (carry, carry_send, carry_recv)):
        for chunk in range(4):
            across_depth(
                buffer.at[chunk, 0], buffer.at[chunk, 1], send.at[0, chunk], recv.at[0, chunk], near
            ).wait_send()
            across_depth(
                buffer.at[chunk, 3], buffer.at[chunk, 2], send.at[1, chunk], recv.at[1, chunk], far
            ).wait_send()
    all_tiles(geo_tx, geo_rx, geo_sem).wait_send()
    all_tiles(feat_tx, feat_rx, feat_sem).wait_send()
    keep_own.wait()
    keep_geo.wait()
    all_tiles(grad_tx, grad_rx, grad_sem).wait()
    all_tiles(ggeo_tx, ggeo_rx, ggeo_sem).wait()


def owner_kernel(picked, grad_rx, ggeo_rx, image, grad_out, ggeo_out, image_out, rows):
    cap, nt = picked.shape
    image_out[...] = image[...]

    def put(t, c):
        for j in range(cap):
            k = t * cap + j
            at = picked[j, t]
            grad_out[at] = grad_rx[k].astype(F32)
            for r in range(2):
                rows[r, pl.ds(at, 1), :] = ggeo_rx[k, r : r + 1, :]
        return c

    lax.fori_loop(0, nt, put, 0, unroll=4)
    for r in range(2):
        turned = jnp.transpose(rows[r])
        for m in range(4 if r == 0 else 2):
            ggeo_out[4 * r + m] = turned[m * 32 : m * 32 + 32]


def local(features, geometry, send_lists, tile_ids, tile_lists, live_counts, cotangent):
    nt, nd = lax.axis_size("tile"), lax.axis_size("depth")
    cap = send_lists.shape[2]
    slots = nt * cap
    blocks = features.shape[0]
    picked = jnp.transpose(send_lists[0])

    vmem = pl.BlockSpec(memory_space=pltpu.VMEM)
    smem = pl.BlockSpec(memory_space=pltpu.SMEM)
    hbm = pl.BlockSpec(memory_space=pl.ANY)
    dma = pltpu.SemaphoreType.DMA
    big = pltpu.VMEM((4, 16, 256, 128), F32)
    image, grad_rx, ggeo_rx = pl.pallas_call(
        functools.partial(splat_kernel, nt, nd, cap),
        out_shape=(
            jax.ShapeDtypeStruct((4, 64, 128), BF16),
            jax.ShapeDtypeStruct((slots, 32, 128), BF16),
            jax.ShapeDtypeStruct((slots, 2, 128), F32),
        ),
        in_specs=[hbm, hbm, smem, smem, smem, smem, hbm],
        out_specs=(vmem, hbm, hbm),
        scratch_shapes=[
            pltpu.VMEM((blocks, 32, 128), BF16),
            pltpu.VMEM((6, blocks, 128), F32),
            pltpu.VMEM((slots, 32, 128), BF16),
            pltpu.VMEM((slots, 32, 128), BF16),
            pltpu.VMEM((16, 256, 128), BF16),
            pltpu.VMEM((2, blocks, 128), F32),
            pltpu.VMEM((slots, 2, 128), F32),
            pltpu.VMEM((slots, 2, 128), F32),
            pltpu.VMEM((nd, 8, 128), I32),
            pltpu.VMEM((8, 128), I32),
            pltpu.SMEM((nd, 8, 128), I32),
            pltpu.SMEM((8, 128), I32),
            pltpu.VMEM((2, 4, 32, 128), F32),
            pltpu.VMEM((6, 32, 128), F32),
            pltpu.VMEM((4, 256, 128), BF16),
            pltpu.VMEM((4, 128, 256), BF16),
            pltpu.VMEM((16, 256, 128), BF16),
            pltpu.VMEM((8, 256, 256), BF16),
            pltpu.VMEM((8, 256, 256), BF16),
            big,
            big,
            big,
            big,
            pltpu.VMEM((4, 8, 256, 256), BF16),
            pltpu.VMEM((256, 128), F32),
            pltpu.VMEM((4, 4, 128, 128), F32),
            pltpu.VMEM((4, 4, 128, 128), F32),
            pltpu.VMEM((256, 256), BF16),
            pltpu.VMEM((8, 128, 256), F32),
            pltpu.VMEM((slots, 32, 128), BF16),
            pltpu.VMEM((slots, 32, 128), BF16),
            pltpu.VMEM((6, 32, 128), F32),
            pltpu.VMEM((slots, 2, 128), F32),
            pltpu.VMEM((slots, 2, 128), F32),
            pltpu.VMEM((2, 2, 2, 128, 128), F32),
            pltpu.VMEM((nd, 2, 2, 64, 128), F32),
            dma((14,)),
            dma((2,)),
            dma((2,)),
            dma((2,)),
            dma((2,)),
            dma((nd,)),
            dma((nd,)),
            dma((2, 4)),
            dma((2, 4)),
            dma((2, 4)),
            dma((2, 4)),
            dma((nd,)),
            dma((nd,)),
        ],
        compiler_params=pltpu.CompilerParams(
            collective_id=0, has_side_effects=True, vmem_limit_bytes=62 * 1024 * 1024
        ),
        name="splat",
    )(
        features,
        jnp.transpose(geometry, (1, 0, 2)),
        picked,
        tile_ids,
        tile_lists,
        jnp.transpose(live_counts),
        cotangent,
    )

    feature_grads, geometry_grads, image_out = pl.pallas_call(
        owner_kernel,
        out_shape=(
            jax.ShapeDtypeStruct((blocks, 32, 128), F32),
            jax.ShapeDtypeStruct((6, 32, blocks), F32),
            jax.ShapeDtypeStruct((4, 64, 128), BF16),
        ),
        in_specs=[smem, vmem, vmem, vmem],
        out_specs=(vmem, vmem, vmem),
        scratch_shapes=[pltpu.VMEM((2, blocks, 128), F32)],
        name="owner",
    )(picked, grad_rx, ggeo_rx, image)
    return image_out, feature_grads, jnp.transpose(geometry_grads, (2, 0, 1))


def solution(mesh):
    placed = (
        P("tile", None, None),
        P("tile", None, None),
        P("tile", None, None),
        P("tile"),
        P("tile", "depth", None),
        P("tile", "depth"),
        P("tile", None, None),
    )
    return jax.shard_map(
        local,
        mesh=mesh,
        in_specs=placed,
        out_specs=(P("tile", "depth", None), P("tile", "depth", None), P("tile", None, "depth")),
        check_vma=False,
    )
```

```python
import functools

import jax
import jax.numpy as jnp
from jax import lax
from jax.experimental import pallas as pl
from jax.experimental.pallas import tpu as pltpu
from jax.sharding import PartitionSpec as P

MESH = pl.DeviceIdType.MESH
F32 = jnp.float32
BF16 = jnp.bfloat16
I32 = jnp.int32


def iota(shape, dim):
    return lax.broadcasted_iota(I32, shape, dim)


def ones_where(mask):
    return jnp.where(mask, 1.0, 0.0).astype(BF16)


def split_two(value):
    high = value.astype(BF16)
    low = (value - high.astype(F32)).astype(BF16)
    return high, low


def group_of(par, g, h):
    return (g // 2) * 8 + par * 4 + (g % 2) * 2 + h


def groups(step, many):
    def several(i, c):
        for k in range(many):
            step(i * many + k, c)
        return c

    lax.fori_loop(0, 8 // many, several, 0)


def chained(first, second, many):
    def several(i, c):
        coming = first(i * many)
        for k in range(many):
            ready = coming
            if k + 1 < many:
                coming = first(i * many + k + 1)
            second(i * many + k, ready)
        return c

    lax.fori_loop(0, 8 // many, several, 0)


def splat_kernel(
    nt,
    nd,
    cap,
    features,
    geometry,
    picked,
    tile_ids,
    tile_lists,
    live_counts,
    cotangent,
    image_out,
    grad_rx,
    ggeo_rx,
    own_feat,
    own_geo,
    feat_tx,
    feat_rx,
    feat_list,
    geo_rows,
    geo_tx,
    geo_rx,
    lists_rx,
    inv_vec,
    lists_sm,
    inv_sm,
    geo_part,
    geo,
    cot,
    cot_turned,
    place_mat,
    ahead_mat,
    behind_mat,
    fall,
    chain,
    thru,
    later,
    weights,
    sums,
    light,
    carry,
    offs,
    grad_sum,
    grad_list,
    grad_tx,
    moment,
    ggeo_list,
    ggeo_tx,
    image_part,
    image_rx,
    local_sem,
    geo_sem,
    feat_sem,
    grad_sem,
    ggeo_sem,
    lists_send,
    lists_recv,
    light_send,
    light_recv,
    carry_send,
    carry_recv,
    image_send,
    image_recv,
):
    me = lax.axis_index("tile")
    my = lax.axis_index("depth")
    slots = nt * cap
    near = my + 1 - 2 * (my % 2)
    far = nd - 1 - my

    def greet(i, c):
        pl.semaphore_signal(
            barrier, inc=1, device_id={"tile": lax.rem(me + i, nt)}, device_id_type=MESH
        )
        return c

    barrier = pltpu.get_barrier_semaphore()
    lax.fori_loop(1, nt, greet, 0)
    for step in range(1, nd):
        pl.semaphore_signal(
            barrier, inc=1, device_id={"depth": lax.rem(my + step, nd)}, device_id_type=MESH
        )

    fetch_geo = pltpu.make_async_copy(geometry, own_geo, local_sem.at[0])
    fetch_geo.start()
    fetch_feat = pltpu.make_async_copy(
        features.at[:, pl.ds(pl.multiple_of(my * 32, 32), 32), :], own_feat, local_sem.at[1]
    )
    fetch_feat.start()
    fetch_cot = []
    for par in range(2):
        for ph in range(2):
            for high in range(2):
                copy = pltpu.make_async_copy(
                    cotangent.at[high * 2 + par, pl.ds(ph * 128, 128), :],
                    cot.at[par * 2 + ph, pl.ds(high * 128, 128), :],
                    local_sem.at[5 + par * 4 + ph * 2 + high],
                )
                copy.start()
                fetch_cot.append(copy)

    lane8 = iota((8, 128), 1)
    listed = jnp.zeros((8, 128), I32)
    for u in range(4):
        for g in range(2):
            for k in range(8):
                listed = jnp.where(lane8 == u * 16 + g * 8 + k, tile_lists[u, g, k], listed)
            listed = jnp.where(lane8 == 64 + u * 2 + g, live_counts[g, u], listed)
    lists_rx[my] = listed

    fetch_geo.wait()
    lane_group = iota((slots, 128), 1) // 32
    for r in range(2):
        total = jnp.zeros((slots, 128), F32)
        for m in range(4 if r == 0 else 2):
            shift = lax.rem(32 * m + 128 - 32 * my, 128)
            total = jnp.where(lane_group == m, pltpu.roll(own_geo[4 * r + m], shift, 1), total)
        geo_rows[r] = total

    def pick_geo(t, c):
        for j in range(cap):
            at = picked[j, t]
            first = geo_rows[0, pl.ds(at, 1), :]
            second = geo_rows[1, pl.ds(at, 1), :]
            geo_tx[t * cap + j] = jnp.concatenate([first, second], axis=0)
        return c

    lax.fori_loop(0, nt, pick_geo, 0, unroll=4)
    mine = pl.multiple_of(me * cap, cap)
    geo_rx[pl.ds(mine, cap)] = geo_tx[pl.ds(mine, cap)]

    def across_depth(source, target, send, recv, peer):
        return pltpu.make_async_remote_copy(
            src_ref=source,
            dst_ref=target,
            send_sem=send,
            recv_sem=recv,
            device_id={"depth": peer},
            device_id_type=MESH,
        )

    def scatter_tiles(source, target, sem):
        def send(i, c):
            peer = lax.rem(me + i, nt)
            there = pl.multiple_of(peer * cap, cap)
            pltpu.make_async_remote_copy(
                src_ref=source.at[pl.ds(there, cap)],
                dst_ref=target.at[pl.ds(mine, cap)],
                send_sem=sem.at[0],
                recv_sem=sem.at[1],
                device_id={"tile": peer},
                device_id_type=MESH,
            ).start()
            return c

        lax.fori_loop(1, nt, send, 0)

    def all_tiles(source, target, sem):
        many = (nt - 1) * cap
        return pltpu.make_async_remote_copy(
            src_ref=source.at[pl.ds(0, many)],
            dst_ref=target.at[pl.ds(0, many)],
            send_sem=sem.at[0],
            recv_sem=sem.at[1],
            device_id={"tile": lax.rem(me + 1, nt)},
            device_id_type=MESH,
        )

    fetch_feat.wait()

    def pick_feat(t, c):
        for j in range(cap):
            feat_tx[t * cap + j] = own_feat[picked[j, t]]
        return c

    lax.fori_loop(0, nt, pick_feat, 0, unroll=4)
    feat_rx[pl.ds(mine, cap)] = feat_tx[pl.ds(mine, cap)]

    row_in = iota((256, 128), 0) % 128
    lane_out = iota((256, 128), 1)
    same_block = row_in // 32 == lane_out // 32
    before_mat = ones_where(same_block & (row_in < lane_out))
    after_mat = ones_where(same_block & (row_in > lane_out))
    place_key = lane_out - row_in // 32
    in_entry = iota((64, 256), 0)
    out_entry = iota((64, 256), 1) // 32

    def build(g, c):
        for h in range(2):
            place_mat[g * 2 + h] = ones_where(place_key == g * 8 + h * 4)
        want = out_entry + g * 8
        equal = ones_where(in_entry == want)
        less = ones_where(in_entry < want)
        more = ones_where(in_entry > want)
        ahead_mat[g] = jnp.concatenate([less, equal, less, equal], axis=0)
        behind_mat[g] = jnp.concatenate([more, equal, more, equal], axis=0)
        return c

    lax.fori_loop(0, 8, build, 0)

    for copy in fetch_cot:
        copy.wait()
    for chunk in range(4):
        cot_turned[chunk] = jnp.transpose(cot[chunk].astype(F32)).astype(BF16)

    pl.semaphore_wait(barrier, nt - 1 + nd - 1)
    for step in range(1, nd):
        peer = lax.rem(my + step, nd)
        across_depth(
            lists_rx.at[my], lists_rx.at[my], lists_send.at[peer], lists_recv.at[my], peer
        ).start()
    scatter_tiles(geo_tx, geo_rx, geo_sem)
    scatter_tiles(feat_tx, feat_rx, feat_sem)

    for step in range(1, nd):
        other = lax.rem(my + step, nd)
        across_depth(
            lists_rx.at[other], lists_rx.at[other], lists_send.at[other], lists_recv.at[other], other
        ).wait_recv()
    to_scalar = pltpu.make_async_copy(lists_rx, lists_sm, local_sem.at[2])
    to_scalar.start()
    slot_of_row = iota((128, 128), 0)
    lane = iota((128, 128), 1)
    found = jnp.zeros((128, 128), I32)
    for q in range(nd):
        row = jnp.broadcast_to(lists_rx[q, 0:1, :], (128, 128))
        hit = (row == slot_of_row) & (lane < 32)
        found = found + jnp.where(hit, lane + 32 * q, 0)
    for shift in (64, 32, 16, 8, 4, 2, 1):
        found = found + pltpu.roll(found, shift, 1)
    inv_vec[...] = jnp.transpose(found)[0:8]
    to_scalar.wait()
    inv_copy = pltpu.make_async_copy(inv_vec, inv_sm, local_sem.at[3])
    inv_copy.start()

    def within(index):
        return jnp.clip(index, 0, slots - 1)

    def slot_at(par, g, k):
        return within(lists_sm[g // 2, 0, par * 16 + (g % 2) * 8 + k])

    def live_at(tile, g):
        return lists_sm[g // 2, 0, 64 + tile * 2 + g % 2]

    all_tiles(geo_tx, geo_rx, geo_sem).wait_recv()

    def sort_geo(at, c):
        for k in range(8):
            rows = geo_rx[slot_at(at // 8, at % 8, k)]
            group = group_of(at // 8, at % 8, k // 4)
            for r in range(2):
                geo_part[r, k % 4, pl.ds(group, 1), :] = rows[r : r + 1, :]
        return c

    lax.fori_loop(0, 16, sort_geo, 0)
    lane_part = iota((32, 128), 1) // 32
    for p in range(6):
        r, m = p // 4, p % 4
        total = jnp.zeros((32, 128), F32)
        for i in range(4):
            shift = (32 * (i - m)) % 128
            part = geo_part[r, i]
            moved = pltpu.roll(part, shift, 1) if shift else part
            total = jnp.where(lane_part == i, moved, total)
        geo[p] = total

    column = iota((16, 128), 0).astype(F32) + 0.5
    entry_lane = iota((16, 128), 1) // 32
    left = iota((128, 128), 1) < 64

    def row_of(p, group):
        return jnp.broadcast_to(geo[p, pl.ds(group, 1), :], (16, 128))

    def origin(tile):
        return 16.0 * tile_ids[tile].astype(F32)

    def start_near(buffer, send, recv, chunk):
        whole = sums[...]
        buffer[chunk, 0] = jnp.where(left, whole[:128], pltpu.roll(whole[128:], 64, 1))
        across_depth(
            buffer.at[chunk, 0], buffer.at[chunk, 1], send.at[0, chunk], recv.at[0, chunk], near
        ).start()

    def start_far(buffer, send, recv, chunk):
        across_depth(
            buffer.at[chunk, 1], buffer.at[chunk, 1], send.at[0, chunk], recv.at[0, chunk], near
        ).wait_recv()
        buffer[chunk, 3] = buffer[chunk, 0] + buffer[chunk, 1]
        across_depth(
            buffer.at[chunk, 3], buffer.at[chunk, 2], send.at[1, chunk], recv.at[1, chunk], far
        ).start()

    def offsets_from(buffer, send, recv, chunk, use_near, use_far):
        across_depth(
            buffer.at[chunk, 2], buffer.at[chunk, 2], send.at[1, chunk], recv.at[1, chunk], far
        ).wait_recv()
        total = buffer[chunk, 3] + buffer[chunk, 2]
        same = use_near * buffer[chunk, 1] + use_far * buffer[chunk, 2]
        for high in range(2):
            if high == 0:
                both = jnp.where(left, total, pltpu.roll(same, 64, 1))
            else:
                both = jnp.where(left, pltpu.roll(total, 64, 1), same)
            top, rest = split_two(both)
            offs[pl.ds(high * 128, 128), :] = jnp.concatenate([top, rest], axis=1)

    odd = jnp.where(my % 2 == 1, 1.0, 0.0)
    upper = jnp.where(my >= 2, 1.0, 0.0)

    def phase_1(par, c):
        for ph in range(2):
            chunk = par * 2 + ph
            sums[...] = jnp.zeros((256, 128), F32)

            def alpha_step(g, c, par=par, ph=ph, chunk=chunk):
                for h in range(2):
                    group = group_of(par, g, h)
                    mean_x, mean_y = row_of(0, group), row_of(1, group)
                    half_a = -0.5 * row_of(2, group)
                    minus_b = -row_of(3, group)
                    half_c = -0.5 * row_of(4, group)
                    opacity = row_of(5, group)
                    highs, lows = [], []
                    for high in range(2):
                        tile = high * 2 + par
                        dx = column - (mean_x - origin(tile))
                        alive = entry_lane + h * 4 < live_at(tile, g)
                        ax = jnp.where(alive, half_a * dx * dx, -1e30)
                        for py in range(8):
                            dy = (py + ph * 8 + 0.5) - mean_y
                            power = dx * (minus_b * dy) + (ax + half_c * dy * dy)
                            falloff = jnp.exp(power)
                            fall[chunk, g * 2 + h, pl.ds(high * 128 + py * 16, 16), :] = falloff
                            top, rest = split_two(jnp.log(1.0 - opacity * falloff))
                            highs.append(top)
                            lows.append(rest)
                    both = jnp.concatenate(
                        [jnp.concatenate(highs, axis=0), jnp.concatenate(lows, axis=0)], axis=1
                    )
                    right = jnp.concatenate([before_mat, place_mat[g * 2 + h]], axis=1)
                    result = jnp.dot(both, right, preferred_element_type=F32)
                    chain[chunk, g * 2 + h] = result[:, :128]
                    sums[...] += result[:, 128:]
                return c

            groups(alpha_step, 4)
            start_near(light, light_send, light_recv, chunk)

            @pl.when(par == 1)
            def _(ph=ph):
                start_far(light, light_send, light_recv, ph)
        return c

    lax.fori_loop(0, 2, phase_1, 0)

    inv_copy.wait()

    def phase_2(par, c):
        for ph in range(2):
            chunk = par * 2 + ph
            @pl.when(par == 1 - ph)
            def _(ph=ph):
                start_far(light, light_send, light_recv, 3 - ph)

            offsets_from(light, light_send, light_recv, chunk, odd, upper)

            def weight_ahead(g):
                return jnp.dot(offs[...], ahead_mat[g], preferred_element_type=F32)

            def weight_step(g, ahead, par=par, ph=ph, chunk=chunk):
                halves = []
                for h in range(2):
                    group = group_of(par, g, h)
                    opacity = jnp.broadcast_to(geo[5, pl.ds(group, 1), :], (256, 128))
                    through = jnp.exp(chain[chunk, g * 2 + h] + ahead[:, h * 128 : (h + 1) * 128])
                    thru[chunk, g * 2 + h] = through
                    halves.append((through * (opacity * fall[chunk, g * 2 + h])).astype(BF16))
                weight = jnp.concatenate(halves, axis=1)
                weights[chunk, g] = weight
                grad = jnp.dot(cot_turned[chunk], weight, preferred_element_type=F32)
                if ph == 0:
                    grad_sum[g] = grad
                else:
                    grad = grad + grad_sum[g]
                    at = (g // 2) * 4 + par * 2 + g % 2
                    grad_list[pl.ds(pl.multiple_of(at * 8, 8), 8)] = jnp.transpose(grad).astype(
                        BF16
                    ).reshape(8, 32, 128)

            chained(weight_ahead, weight_step, 4)
        return c

    lax.fori_loop(0, 2, phase_2, 0)

    def back_feat(k, c):
        grad_tx[k] = grad_list[within(inv_sm[0, k])]
        return c

    lax.fori_loop(0, slots, back_feat, 0, unroll=8)
    keep_own = pltpu.make_async_copy(
        grad_tx.at[pl.ds(mine, cap)], grad_rx.at[pl.ds(mine, cap)], local_sem.at[4]
    )
    keep_own.start()
    scatter_tiles(grad_tx, grad_rx, grad_sem)
    all_tiles(feat_tx, feat_rx, feat_sem).wait_recv()

    def sort_feat(at, c):
        for k in range(8):
            feat_list[at, pl.ds(k * 32, 32), :] = feat_rx[slot_at(at // 8, at % 8, k)]
        return c

    lax.fori_loop(0, 16, sort_feat, 0)
    image_part[...] = jnp.zeros(image_part.shape, F32)

    def phase_3(par, c):
        for ph in range(2):
            chunk = par * 2 + ph
            sums[...] = jnp.zeros((256, 128), F32)

            def carry_ahead(g, par=par, ph=ph, chunk=chunk):
                feat = feat_list[par * 8 + g]
                shown = jnp.dot(weights[chunk, g], feat, preferred_element_type=F32)
                image_part[par, ph] += shown.reshape(2, 128, 128)
                return lax.dot_general(
                    cot[chunk], feat, (((1,), (1,)), ((), ())), preferred_element_type=F32
                )

            def carry_step(g, dots, par=par, chunk=chunk):
                for h in range(2):
                    group = group_of(par, g, h)
                    opacity = jnp.broadcast_to(geo[5, pl.ds(group, 1), :], (256, 128))
                    direct = dots[:, h * 128 : (h + 1) * 128] * thru[chunk, g * 2 + h]
                    chain[chunk, g * 2 + h] = direct
                    top, rest = split_two(direct * (opacity * fall[chunk, g * 2 + h]))
                    both = jnp.concatenate([top, rest], axis=1)
                    right = jnp.concatenate([after_mat, place_mat[g * 2 + h]], axis=1)
                    result = jnp.dot(both, right, preferred_element_type=F32)
                    later[chunk, g * 2 + h] = result[:, :128]
                    sums[...] += result[:, 128:]

            chained(carry_ahead, carry_step, 4)
            start_near(carry, carry_send, carry_recv, chunk)
            if ph:
                start_far(carry, carry_send, carry_recv, par * 2)
            else:

                @pl.when(par == 1)
                def _():
                    start_far(carry, carry_send, carry_recv, 1)
        return c

    lax.fori_loop(0, 2, phase_3, 0)

    def phase_4(par, c):
        for ph in range(2):
            chunk = par * 2 + ph
            if ph:

                @pl.when(par == 0)
                def _():
                    start_far(carry, carry_send, carry_recv, 3)
                    for step in range(1, nd):
                        peer = lax.rem(my + step, nd)
                        across_depth(
                            image_part.at[
                                :, peer // 2, :, pl.ds(pl.multiple_of((peer % 2) * 64, 64), 64), :
                            ],
                            image_rx.at[my],
                            image_send.at[peer],
                            image_recv.at[my],
                            peer,
                        ).start()

            offsets_from(carry, carry_send, carry_recv, chunk, 1.0 - odd, 1.0 - upper)

            def shape_step(g, c, par=par, ph=ph, chunk=chunk):
                behind = jnp.dot(offs[...], behind_mat[g], preferred_element_type=F32)
                for h in range(2):
                    group = group_of(par, g, h)
                    mean_x, mean_y = row_of(0, group), row_of(1, group)
                    opacity = row_of(5, group)
                    parts = [jnp.zeros((16, 128), F32) for _ in range(6)]
                    for high in range(2):
                        tile = high * 2 + par
                        dx = column - (mean_x - origin(tile))
                        flat = jnp.zeros((16, 128), F32)
                        tilt = jnp.zeros((16, 128), F32)
                        bend = jnp.zeros((16, 128), F32)
                        for py in range(8):
                            at = high * 128 + py * 16
                            rows = pl.ds(at, 16)
                            dy = (py + ph * 8 + 0.5) - mean_y
                            falloff = fall[chunk, g * 2 + h, rows, :]
                            after = (
                                later[chunk, g * 2 + h, rows, :]
                                + behind[at : at + 16, h * 128 : (h + 1) * 128]
                            )
                            alpha_grad = chain[chunk, g * 2 + h, rows, :] - after / (
                                1.0 - opacity * falloff
                            )
                            term = alpha_grad * falloff
                            term_y = term * dy
                            flat = flat + term
                            tilt = tilt + term_y
                            bend = bend + term_y * dy
                        flat_x = flat * dx
                        adds = [flat, flat_x, tilt, flat_x * dx, tilt * dx, bend]
                        parts = [a + b for a, b in zip(parts, adds)]
                    for i, part in enumerate(parts):
                        folded = jnp.sum(part, axis=0, keepdims=True)
                        if ph:
                            folded = folded + moment[i, pl.ds(group, 1), :]
                        moment[i, pl.ds(group, 1), :] = folded
                return c

            groups(shape_step, 4)
        return c

    lax.fori_loop(0, 2, phase_4, 0)

    one, sx, sy, sxx, sxy, syy = [moment[i] for i in range(6)]
    conic_a, conic_b, conic_c, opac = [geo[p] for p in (2, 3, 4, 5)]
    ggeo = [
        opac * (conic_a * sx + conic_b * sy),
        opac * (conic_b * sx + conic_c * sy),
        -0.5 * opac * sxx,
        -opac * sxy,
        -0.5 * opac * syy,
        one,
    ]
    for i in range(4):
        for r in range(2):
            total = jnp.zeros((32, 128), F32)
            for m in range(4 if r == 0 else 2):
                shift = (32 * (m - i)) % 128
                part = ggeo[4 * r + m]
                moved = pltpu.roll(part, shift, 1) if shift else part
                total = jnp.where(lane_part == m, moved, total)
            for group in range(32):
                ggeo_list[group * 4 + i, r : r + 1, :] = total[group : group + 1]

    def back_geo(k, c):
        ggeo_tx[k] = ggeo_list[within(inv_sm[0, k])]
        return c

    lax.fori_loop(0, slots, back_geo, 0, unroll=8)
    keep_geo = pltpu.make_async_copy(
        ggeo_tx.at[pl.ds(mine, cap)], ggeo_rx.at[pl.ds(mine, cap)], local_sem.at[13]
    )
    keep_geo.start()
    scatter_tiles(ggeo_tx, ggeo_rx, ggeo_sem)

    image = image_part[:, my // 2, :, pl.ds(pl.multiple_of((my % 2) * 64, 64), 64), :]
    for step in range(1, nd):
        other = lax.rem(my + step, nd)
        across_depth(
            image_rx.at[other], image_rx.at[other], image_send.at[other], image_recv.at[other], other
        ).wait_recv()
        image = image + image_rx[other]
    for par in range(2):
        for high in range(2):
            image_out[high * 2 + par] = image[par, high].astype(BF16)

    for step in range(1, nd):
        other = lax.rem(my + step, nd)
        across_depth(
            lists_rx.at[other], lists_rx.at[other], lists_send.at[other], lists_recv.at[other], other
        ).wait_send()
        across_depth(
            image_rx.at[other], image_rx.at[other], image_send.at[other], image_recv.at[other], other
        ).wait_send()
    for buffer, send, recv in ((light, light_send, light_recv), (carry, carry_send, carry_recv)):
        for chunk in range(4):
            across_depth(
                buffer.at[chunk, 0], buffer.at[chunk, 1], send.at[0, chunk], recv.at[0, chunk], near
            ).wait_send()
            across_depth(
                buffer.at[chunk, 3], buffer.at[chunk, 2], send.at[1, chunk], recv.at[1, chunk], far
            ).wait_send()
    all_tiles(geo_tx, geo_rx, geo_sem).wait_send()
    all_tiles(feat_tx, feat_rx, feat_sem).wait_send()
    keep_own.wait()
    keep_geo.wait()
    all_tiles(grad_tx, grad_rx, grad_sem).wait()
    all_tiles(ggeo_tx, ggeo_rx, ggeo_sem).wait()


def owner_kernel(picked, grad_rx, ggeo_rx, image, grad_out, ggeo_out, image_out, held, wide, rows, sems):
    cap, nt = picked.shape
    parts = 4
    many = nt // parts
    fetches = []
    for part in range(parts):
        span = pl.ds(part * many * cap, many * cap)
        fetch = pltpu.make_async_copy(grad_rx.at[span], held.at[span], sems.at[part])
        fetch.start()
        fetches.append(fetch)
    image_out[...] = image[...]

    def widen(t, c):
        for j in range(cap):
            k = t * cap + j
            wide[k] = held[k].astype(F32)
        return c

    def put(t, c):
        for j in range(cap):
            k = t * cap + j
            at = picked[j, t]
            pltpu.make_async_copy(wide.at[k], grad_out.at[at], sems.at[parts]).start()
            for r in range(2):
                rows[r, pl.ds(at, 1), :] = ggeo_rx[k, r : r + 1, :]
        return c

    for part in range(parts):
        fetches[part].wait()
        lax.fori_loop(part * many, part * many + many, widen, 0, unroll=4)
        lax.fori_loop(part * many, part * many + many, put, 0, unroll=4)
    for r in range(2):
        turned = jnp.transpose(rows[r])
        for m in range(4 if r == 0 else 2):
            ggeo_out[4 * r + m] = turned[m * 32 : m * 32 + 32]
    pltpu.make_async_copy(wide, grad_out, sems.at[parts]).wait()


def local(features, geometry, send_lists, tile_ids, tile_lists, live_counts, cotangent):
    nt, nd = lax.axis_size("tile"), lax.axis_size("depth")
    cap = send_lists.shape[2]
    slots = nt * cap
    blocks = features.shape[0]
    picked = jnp.transpose(send_lists[0])

    vmem = pl.BlockSpec(memory_space=pltpu.VMEM)
    smem = pl.BlockSpec(memory_space=pltpu.SMEM)
    hbm = pl.BlockSpec(memory_space=pl.ANY)
    dma = pltpu.SemaphoreType.DMA
    big = pltpu.VMEM((4, 16, 256, 128), F32)
    image, grad_rx, ggeo_rx = pl.pallas_call(
        functools.partial(splat_kernel, nt, nd, cap),
        out_shape=(
            jax.ShapeDtypeStruct((4, 64, 128), BF16),
            jax.ShapeDtypeStruct((slots, 32, 128), BF16),
            jax.ShapeDtypeStruct((slots, 2, 128), F32),
        ),
        in_specs=[hbm, hbm, smem, smem, smem, smem, hbm],
        out_specs=(vmem, hbm, hbm),
        scratch_shapes=[
            pltpu.VMEM((blocks, 32, 128), BF16),
            pltpu.VMEM((6, blocks, 128), F32),
            pltpu.VMEM((slots, 32, 128), BF16),
            pltpu.VMEM((slots, 32, 128), BF16),
            pltpu.VMEM((16, 256, 128), BF16),
            pltpu.VMEM((2, blocks, 128), F32),
            pltpu.VMEM((slots, 2, 128), F32),
            pltpu.VMEM((slots, 2, 128), F32),
            pltpu.VMEM((nd, 8, 128), I32),
            pltpu.VMEM((8, 128), I32),
            pltpu.SMEM((nd, 8, 128), I32),
            pltpu.SMEM((8, 128), I32),
            pltpu.VMEM((2, 4, 32, 128), F32),
            pltpu.VMEM((6, 32, 128), F32),
            pltpu.VMEM((4, 256, 128), BF16),
            pltpu.VMEM((4, 128, 256), BF16),
            pltpu.VMEM((16, 256, 128), BF16),
            pltpu.VMEM((8, 256, 256), BF16),
            pltpu.VMEM((8, 256, 256), BF16),
            big,
            big,
            big,
            big,
            pltpu.VMEM((4, 8, 256, 256), BF16),
            pltpu.VMEM((256, 128), F32),
            pltpu.VMEM((4, 4, 128, 128), F32),
            pltpu.VMEM((4, 4, 128, 128), F32),
            pltpu.VMEM((256, 256), BF16),
            pltpu.VMEM((8, 128, 256), F32),
            pltpu.VMEM((slots, 32, 128), BF16),
            pltpu.VMEM((slots, 32, 128), BF16),
            pltpu.VMEM((6, 32, 128), F32),
            pltpu.VMEM((slots, 2, 128), F32),
            pltpu.VMEM((slots, 2, 128), F32),
            pltpu.VMEM((2, 2, 2, 128, 128), F32),
            pltpu.VMEM((nd, 2, 2, 64, 128), F32),
            dma((14,)),
            dma((2,)),
            dma((2,)),
            dma((2,)),
            dma((2,)),
            dma((nd,)),
            dma((nd,)),
            dma((2, 4)),
            dma((2, 4)),
            dma((2, 4)),
            dma((2, 4)),
            dma((nd,)),
            dma((nd,)),
        ],
        compiler_params=pltpu.CompilerParams(
            collective_id=0, has_side_effects=True, vmem_limit_bytes=62 * 1024 * 1024
        ),
        name="splat",
    )(
        features,
        jnp.transpose(geometry, (1, 0, 2)),
        picked,
        tile_ids,
        tile_lists,
        jnp.transpose(live_counts),
        cotangent,
    )

    feature_grads, geometry_grads, image_out = pl.pallas_call(
        owner_kernel,
        out_shape=(
            jax.ShapeDtypeStruct((blocks, 32, 128), F32),
            jax.ShapeDtypeStruct((6, 32, blocks), F32),
            jax.ShapeDtypeStruct((4, 64, 128), BF16),
        ),
        in_specs=[smem, hbm, vmem, vmem],
        out_specs=(hbm, vmem, vmem),
        scratch_shapes=[
            pltpu.VMEM((slots, 32, 128), BF16),
            pltpu.VMEM((slots, 32, 128), F32),
            pltpu.VMEM((2, blocks, 128), F32),
            dma((5,)),
        ],
        name="owner",
    )(picked, grad_rx, ggeo_rx, image)
    return image_out, feature_grads, jnp.transpose(geometry_grads, (2, 0, 1))


def solution(mesh):
    placed = (
        P("tile", None, None),
        P("tile", None, None),
        P("tile", None, None),
        P("tile"),
        P("tile", "depth", None),
        P("tile", "depth"),
        P("tile", None, None),
    )
    return jax.shard_map(
        local,
        mesh=mesh,
        in_specs=placed,
        out_specs=(P("tile", "depth", None), P("tile", "depth", None), P("tile", None, "depth")),
        check_vma=False,
    )
```
